32 devices in a mesh: row: 8 (over z, core), col: 4 (over y, x).
Axes of the slice: x: 2, y: 2, z: 4, core: 2. Of those that a mesh axis runs over, the one named last changes fastest.
Arguments:
- mode_basis: bfloat16 [4096, 4096], P('row'), may hold values from -0.125 to 0.125
- node_coords: float32 [3, 4096], P(None, 'row'), may hold values from -1 to 1
- quad_weights: float32 [4096], P('row'), may hold values from 0.3 to 3
- magnetization: bfloat16 [2, 4096, 32], P(None, 'col', 'row'), may hold values from -6 to 6
- decay_rates: float32 [4096], replicated, may hold values from 0.02 to 1.5
- directions: float32 [6, 3, 32], replicated, may hold values from -3 to 3
Outputs:
- final_magnet: bfloat16 [2, 4096, 32], P(None, 'col', 'row')
The draws below stay inside these ranges and needn't reach their ends.
All inputs are finite; a program needn't handle non-finite values.
Results may differ from the reference program's by a relative error of at most 0.03.
Values may be sent and summed in bfloat16 or wider, within the bound.
A program may use at most 64 MiB of HBM per device.

```python
import math
import jax
import jax.numpy as jnp
from jax import lax

MODES = 4096
STEPS = 3
NODES = 4096
WAVEFORMS = 32
N_ROW = 8


def strengthened(drawn, own_key, source, target, blocks, factor):
    owner, partner = [(jnp.arange(drawn.shape[position]) // (drawn.shape[position] // blocks)).reshape([-1 if axis == position else 1 for axis in range(drawn.ndim)]) for position in (source, target)]
    chosen = jax.random.permutation(own_key, blocks)[partner]
    strong = (owner == chosen) | (owner == (partner + blocks // 2) % blocks)
    return jnp.where(strong, factor * drawn, drawn)


def shard_levels(rng, dims, cuts, low, largest):
    gain, own = 1.0, jax.random.fold_in(rng, 6)
    for position, parts in cuts:
        heights = jnp.exp(jax.random.uniform(jax.random.fold_in(own, position), (parts,), jnp.float32, low / len(cuts), largest / len(cuts)))
        gain = gain * jnp.repeat(heights, dims[position] // parts).reshape([-1 if axis == position else 1 for axis in range(len(dims))])
    return gain


def normal_values(key, extent, scale, bound, cuts=(), kind=jnp.bfloat16):
    entries = jax.random.normal(key, extent, jnp.float32) * scale
    if len(cuts) > 0:
        entries = shard_levels(key, extent, cuts, -0.22, 0.18) * entries
    return jnp.clip(entries, min=-bound, max=bound).astype(kind)


def bell_draw_with(own_key, shape, spread, limit, cuts, heavy, kind=jnp.bfloat16):
    array = spread * jax.random.normal(own_key, shape, jnp.float32)
    if cuts:
        array = array * shard_levels(own_key, shape, cuts, -0.22, 0.18)
    return jnp.clip(strengthened(array, jax.random.fold_in(own_key, 3), *heavy), -limit, limit).astype(kind)


def setup_inputs(seed: int = 0) -> dict:
    arg_keys = jax.random.split(jax.random.key(seed), 7)
    return {
        "mode_basis": bell_draw_with(arg_keys[0], (NODES, MODES), NODES ** -0.5, 0.125, ((0, 8),), (0, 1, 8, 2.0)),
        "node_coords": jnp.clip(jax.random.uniform(arg_keys[1], (3, NODES), jnp.float32, -1.0, 1.0) * shard_levels(arg_keys[1], (3, NODES), ((1, 8),), -0.4, 0.0), -1.0, 1.0),
        "quad_weights": jnp.clip(jnp.exp(math.log(3.0) - 2.3025851 * jax.random.uniform(arg_keys[2], (NODES,), jnp.float32) ** shard_levels(arg_keys[2], (NODES,), ((0, 8),), -0.2, 0.2)), 0.3, 3.0),
        "magnetization": normal_values(arg_keys[3], (2, MODES, WAVEFORMS), 1.0, 6.0, ((1, 4), (2, 8))),
        "decay_rates": jnp.clip(jnp.exp(jax.random.uniform(arg_keys[4], (MODES,), jnp.float32, math.log(0.02), math.log(1.5))), 0.02, 1.5),
        "directions": normal_values(arg_keys[5], (2 * STEPS, 3, WAVEFORMS), 0.5, 3.0, (), jnp.float32),
    }


def reference(mode_basis, node_coords, quad_weights, magnetization, decay_rates, directions):
    moments = node_coords * quad_weights[None, :]
    slab_rows = NODES // N_ROW

    def add_slab(accum, slab_index):
        first_node = slab_index * slab_rows
        basis_slab = lax.dynamic_slice_in_dim(mode_basis, first_node, slab_rows, 0)
        moment_slab = lax.dynamic_slice_in_dim(moments, first_node, slab_rows, 1)
        pieces = []
        for axis_index in range(3):
            weighted = (basis_slab.astype(jnp.float32) * moment_slab[axis_index][:, None]).astype(jnp.bfloat16)
            partial_gram = lax.dot_general(basis_slab, weighted, (((0,), (0,)), ((), ())), preferred_element_type=jnp.float32)
            rounded = lax.optimization_barrier(partial_gram.astype(jnp.bfloat16))
            pieces.append(rounded.astype(jnp.float32))
        return accum + jnp.stack(pieces), None

    total_gram, _ = lax.scan(add_slab, jnp.zeros((3, MODES, MODES), jnp.float32), jnp.arange(N_ROW, dtype=jnp.int32))
    moment_gram = total_gram.astype(jnp.bfloat16)

    def apply_operator(field_now, weights_now, factor, keep_part):
        joined = jnp.concatenate([field_now[0], field_now[1]], axis=1)
        combined = jnp.zeros((MODES, 2 * WAVEFORMS), jnp.float32)
        for axis_index in range(3):
            scale_row = jnp.concatenate([weights_now[axis_index], weights_now[axis_index]])
            combined = combined + scale_row[None, :] * jnp.dot(moment_gram[axis_index], joined, preferred_element_type=jnp.float32)
        real_q = combined[:, :WAVEFORMS]
        imag_q = combined[:, WAVEFORMS:]
        diag_scale = (keep_part - factor * decay_rates)[:, None]
        field_float = field_now.astype(jnp.float32)
        new_real = factor * imag_q + diag_scale * field_float[0]
        new_imag = -factor * real_q + diag_scale * field_float[1]
        return jnp.stack([new_real, new_imag])

    field_now = magnetization
    for step_index in range(STEPS):
        half_field = apply_operator(field_now, directions[2 * step_index], 0.5, 1.0).astype(jnp.bfloat16)
        update = apply_operator(half_field, directions[2 * step_index + 1], 1.0, 0.0)
        field_now = (field_now.astype(jnp.float32) + update).astype(jnp.bfloat16)
    return field_now
```

```python
import functools

import jax
import jax.numpy as jnp
from jax import lax
from jax.experimental import pallas as pl
from jax.experimental.pallas import tpu as pltpu
from jax.sharding import PartitionSpec as P

STEPS = 3
CHUNK = 512
SLAB_PIECES = 4
MESH = pl.DeviceIdType.MESH
NT = (((1,), (1,)), ((), ()))
NN = (((1,), (0,)), ((), ()))


def kernel(
    R, C, basis_hbm, coords, quad, start, rates, dirs, out,
    basis, landed, cur, field, lam, parts, recv, weights, coords_in, quad_in, scaled,
    lastout, lastin,
    basis_sem, slab_send, slab_recv, geo_send, geo_recv, first_send, first_recv,
    part_send, part_recv, last_send, last_recv,
):
    H = R // C
    G = R // H
    r = lax.axis_index("row")
    c = lax.axis_index("col")
    z = r // H
    q = lax.rem(r, H)
    wl, width = start.shape[1], start.shape[2]
    rows = 2 * wl
    local = basis_hbm.shape[0]
    M = basis_hbm.shape[1]
    halves = 2 * STEPS
    chunks = M // CHUNK

    own_copy = pltpu.make_async_copy(basis_hbm, basis.at[pl.ds(0, local), :], basis_sem)
    own_copy.start()

    barrier = pltpu.get_barrier_semaphore()
    is_self = z == c

    def greet(row, col):
        pl.semaphore_signal(barrier, inc=1, device_id=(row, col), device_id_type=MESH)

    def unless(cond, fn):
        pl.when(jnp.logical_not(cond))(fn)

    for d in reversed(range(C)):
        unless(is_self & (d == 0), functools.partial(greet, H * c + q, c ^ d))
    for d in reversed(range(G)):
        unless(is_self & (d == 0), functools.partial(greet, H * (z ^ d) + q, z))
    for d in range(1, G):
        greet(H * (z ^ d) + q, c)
    for d in range(1, H):
        greet(H * z + (q ^ d), c)

    row_id = lax.broadcasted_iota(jnp.int32, (rows, dirs.shape[2]), 0)
    wave_id = lax.broadcasted_iota(jnp.int32, (rows, dirs.shape[2]), 1)
    chosen = wave_id == (H * c + q) * wl + row_id % wl

    def fill_weights(slot, xyz, qw):
        for a in range(halves):
            column = [
                (1.0 if a % 2 else 0.5)
                * jnp.sum(jnp.where(chosen, dirs[a, k : k + 1, :], 0.0), axis=1, keepdims=True)
                for k in range(3)
            ]
            for i in range(local // 128):
                lanes = pl.ds(i * 128, 128)
                w = qw[i : i + 1, :]
                weights[a, :, pl.ds(slot * local + i * 128, 128)] = (
                    column[0] * (xyz[0:1, lanes] * w)
                    + column[1] * (xyz[1:2, lanes] * w)
                    + column[2] * (xyz[2:3, lanes] * w)
                )

    fill_weights(0, coords, quad)
    for i in range(M // 128):
        lam[:, pl.ds(i * 128, 128)] = jnp.broadcast_to(rates[i : i + 1, :], (rows, 128))

    pl.semaphore_wait(barrier, C + 2 * G - 1 + H - 1 - 2 * is_self.astype(jnp.int32))

    def first_copy(d):
        return pltpu.make_async_remote_copy(
            src_ref=start, dst_ref=landed.at[c], send_sem=first_send.at[d],
            recv_sem=first_recv.at[c], device_id=(H * (z ^ d) + q, z), device_id_type=MESH,
        )

    for d in reversed(range(G)):
        unless(is_self & (d == 0), lambda d=d: first_copy(d).start())

    @pl.when(is_self)
    def _():
        pltpu.make_async_copy(start, landed.at[c], first_recv.at[c]).start()

    piece = local // SLAB_PIECES

    def geo_copy(d, which):
        src, dst = ((coords, coords_in), (quad, quad_in))[which]
        return pltpu.make_async_remote_copy(
            src_ref=src, dst_ref=dst.at[d - 1], send_sem=geo_send.at[d - 1, which],
            recv_sem=geo_recv.at[d - 1, which], device_id=(H * z + (q ^ d), c),
            device_id_type=MESH,
        )

    def slab_copy(d, j):
        return pltpu.make_async_remote_copy(
            src_ref=basis_hbm.at[pl.ds(j * piece, piece), :],
            dst_ref=basis.at[pl.ds(d * local + j * piece, piece), :],
            send_sem=slab_send.at[d - 1, j], recv_sem=slab_recv.at[d - 1, j],
            device_id=(H * z + (q ^ d), c), device_id_type=MESH,
        )

    for d in range(1, H):
        for which in range(2):
            geo_copy(d, which).start()
        for j in range(SLAB_PIECES):
            slab_copy(d, j).start()
    for d in range(1, H):
        for which in range(2):
            geo_copy(d, which).wait_recv()
        fill_weights(d, coords_in.at[d - 1], quad_in.at[d - 1])

    for s in range(C):
        pltpu.make_async_copy(start, landed.at[s], first_recv.at[s]).wait()
        for x in range(2):
            field[pl.ds(x * wl, wl), pl.ds(s * width, width)] = landed[s, x].astype(jnp.float32)
    cur[...] = field[...].astype(jnp.bfloat16)
    own_copy.wait()

    part_id = lax.broadcasted_iota(jnp.int32, (rows, local), 0) // wl

    def scale(total, a, slot):
        lanes = pl.ds(slot * local, local)
        v = total * weights[a, :, lanes]
        turned = jnp.where(part_id == 0, pltpu.roll(v, rows - wl, 0), -pltpu.roll(v, wl, 0))
        scaled[:, lanes] = turned.astype(jnp.bfloat16)

    scale(
        lax.dot_general(
            cur[...], basis[pl.ds(0, local), :], NT, preferred_element_type=jnp.float32
        ), 0, 0,
    )
    for d in range(1, H):
        pieces = []
        for j in range(SLAB_PIECES):
            slab_copy(d, j).wait_recv()
            pieces.append(lax.dot_general(
                cur[...], basis[pl.ds(d * local + j * piece, piece), :], NT,
                preferred_element_type=jnp.float32,
            ))
        scale(jnp.concatenate(pieces, axis=1), 0, d)

    def part_copy(p, d, i):
        return pltpu.make_async_remote_copy(
            src_ref=parts.at[p, i], dst_ref=recv.at[p, d - 1, i],
            send_sem=part_send.at[p, d - 1, i], recv_sem=part_recv.at[p, d - 1, i],
            device_id=(H * (z ^ d) + q, c), device_id_type=MESH,
        )

    def half_step(step, carry):
        p = lax.rem(step, 2)
        odd = p == 1
        factor = jnp.where(odd, 1.0, 0.5).astype(jnp.float32)
        v = scaled[...]
        for i in range(chunks):
            parts[p, i] = lax.dot_general(
                v, basis[:, pl.ds(i * CHUNK, CHUNK)], NN, preferred_element_type=jnp.float32
            ).astype(jnp.bfloat16)
            for d in reversed(range(1, G)):
                part_copy(p, d, i).start()
        total = jnp.zeros((rows, H * local), jnp.float32)
        for i in range(chunks):
            lanes = pl.ds(i * CHUNK, CHUNK)
            old = field[:, lanes]
            acc = old - (factor * lam[:, lanes]) * cur[:, lanes].astype(jnp.float32)
            acc = acc + parts[p, i].astype(jnp.float32)
            for d in range(1, G):
                part_copy(p, d, i).wait_recv()
                acc = acc + recv[p, d - 1, i].astype(jnp.float32)
            rounded = acc.astype(jnp.bfloat16)
            cur[:, lanes] = rounded
            field[:, lanes] = jnp.where(odd, rounded.astype(jnp.float32), old)
            total = total + lax.dot_general(
                rounded, basis[:, lanes], NT, preferred_element_type=jnp.float32
            )
        for slot in range(H):
            scale(total[:, slot * local : (slot + 1) * local], step + 1, slot)
        for i in range(chunks):
            for d in range(1, G):
                part_copy(p, d, i).wait_send()
        return carry

    lax.fori_loop(0, halves - 1, half_step, 0)

    def last_copy(d):
        return pltpu.make_async_remote_copy(
            src_ref=lastout.at[d], dst_ref=lastin.at[z], send_sem=last_send.at[d],
            recv_sem=last_recv.at[z], device_id=(H * c + q, c ^ d), device_id_type=MESH,
        )

    v = scaled[...]
    for d in reversed(range(C)):
        lanes = pl.ds(pl.multiple_of((c ^ d) * width, width), width)
        rest = field[:, lanes] - lam[:, lanes] * cur[:, lanes].astype(jnp.float32)
        block = lax.dot_general(v, basis[:, lanes], NN, preferred_element_type=jnp.float32)
        lastout[d] = (block + jnp.where(is_self, rest, 0.0)).astype(jnp.bfloat16)
        if d:
            last_copy(d).start()
    unless(is_self, lambda: last_copy(0).start())

    @pl.when(is_self)
    def _():
        pltpu.make_async_copy(lastout.at[0], lastin.at[z], last_recv.at[z]).start()

    fresh = jnp.zeros((rows, width), jnp.float32)
    for s in range(G):
        pltpu.make_async_copy(lastout.at[0], lastin.at[s], last_recv.at[s]).wait()
        fresh = fresh + lastin[s].astype(jnp.float32)
    for x in range(2):
        out[x] = fresh[x * wl : (x + 1) * wl, :].astype(jnp.bfloat16)

    for d in range(C):
        unless(is_self & (d == 0), lambda d=d: last_copy(d).wait_send())
    for d in range(G):
        unless(is_self & (d == 0), lambda d=d: first_copy(d).wait_send())
    for d in range(1, H):
        for which in range(2):
            geo_copy(d, which).wait_send()
        for j in range(SLAB_PIECES):
            slab_copy(d, j).wait_send()


def on_device(R, C, basis, coords, quad, magnetization, rates, dirs):
    H = R // C
    G = R // H
    local, M = basis.shape
    start = jnp.transpose(magnetization, (0, 2, 1))
    _, wl, width = start.shape
    rows = 2 * wl
    chunks = M // CHUNK
    vmem = pl.BlockSpec(memory_space=pltpu.VMEM)
    dma = pltpu.SemaphoreType.DMA
    bf16, f32 = jnp.bfloat16, jnp.float32
    result = pl.pallas_call(
        functools.partial(kernel, R, C),
        out_shape=jax.ShapeDtypeStruct(start.shape, bf16),
        in_specs=[pl.BlockSpec(memory_space=pl.ANY)] + [vmem] * 5,
        out_specs=vmem,
        scratch_shapes=[
            pltpu.VMEM((H * local, M), bf16),
            pltpu.VMEM((C, 2, wl, width), bf16),
            pltpu.VMEM((rows, M), bf16),
            pltpu.VMEM((rows, M), f32),
            pltpu.VMEM((rows, M), f32),
            pltpu.VMEM((2, chunks, rows, CHUNK), bf16),
            pltpu.VMEM((2, G - 1, chunks, rows, CHUNK), bf16),
            pltpu.VMEM((2 * STEPS, rows, H * local), f32),
            pltpu.VMEM((H - 1, 3, local), f32),
            pltpu.VMEM((H - 1, local // 128, 128), f32),
            pltpu.VMEM((rows, H * local), bf16),
            pltpu.VMEM((C, rows, width), bf16),
            pltpu.VMEM((G, rows, width), bf16),
            dma,
            dma((H - 1, SLAB_PIECES)), dma((H - 1, SLAB_PIECES)),
            dma((H - 1, 2)), dma((H - 1, 2)),
            dma((G,)), dma((C,)),
            dma((2, G - 1, chunks)), dma((2, G - 1, chunks)),
            dma((C,)), dma((G,)),
        ],
        compiler_params=pltpu.CompilerParams(collective_id=0, has_side_effects=True),
    )(basis, coords, quad.reshape(-1, 128), start, rates.reshape(-1, 128), dirs)
    return jnp.transpose(result, (0, 2, 1))


def solution(mesh):
    return jax.shard_map(
        functools.partial(on_device, mesh.shape["row"], mesh.shape["col"]),
        mesh=mesh,
        in_specs=(P("row", None), P(None, "row"), P("row"), P(None, "col", "row"), P(), P()),
        out_specs=P(None, "col", "row"),
        check_vma=False,
    )
```

```python
import functools

import jax
import jax.numpy as jnp
from jax import lax
from jax.experimental import pallas as pl
from jax.experimental.pallas import tpu as pltpu
from jax.sharding import PartitionSpec as P

STEPS = 3
CHUNK = 512
MESH = pl.DeviceIdType.MESH
NT = (((1,), (1,)), ((), ()))
NN = (((1,), (0,)), ((), ()))


def kernel(
    R, C, basis_hbm, coords_hbm, quad_hbm, start, rates_hbm, dirs_hbm, out,
    basis, coords, quad, rates, dirs, landed, cur, field, both, lam, early, parts, recv, weights,
    coords_in, quad_in, nodes_out, nodes_in, scaled, lastout, lastin,
    load_sem, slab_send, slab_recv, geo_send, geo_recv, first_send, first_recv,
    node_send, node_recv, part_send, part_recv, last_send, last_recv,
):
    H = R // C
    G = R // H
    r = lax.axis_index("row")
    c = lax.axis_index("col")
    z = r // H
    q = lax.rem(r, H)
    wl, width = start.shape[1], start.shape[2]
    rows = 2 * wl
    local = basis_hbm.shape[0]
    M = basis_hbm.shape[1]
    halves = 2 * STEPS
    chunks = M // CHUNK

    barrier = pltpu.get_barrier_semaphore()
    is_self = z == c

    def greet(row, col):
        pl.semaphore_signal(barrier, inc=1, device_id=(row, col), device_id_type=MESH)

    def unless(cond, fn):
        pl.when(jnp.logical_not(cond))(fn)

    for d in reversed(range(C)):
        for e in range(H):
            unless(is_self & (d + e == 0), functools.partial(greet, H * c + (q ^ e), c ^ d))
    for d in reversed(range(G)):
        for e in range(H):
            unless(is_self & (d + e == 0), functools.partial(greet, H * (z ^ d) + (q ^ e), z))
    for d in range(1, G):
        greet(H * (z ^ d) + q, c)
    for e in range(1, H):
        greet(H * z + (q ^ e), c)

    loads = [
        pltpu.make_async_copy(src, dst, load_sem.at[k])
        for k, (src, dst) in enumerate((
            (coords_hbm, coords), (quad_hbm, quad), (rates_hbm, rates), (dirs_hbm, dirs),
            (basis_hbm, basis.at[pl.ds(0, local), :]),
        ))
    ]
    for load in loads:
        load.start()
    for load in loads[:-1]:
        load.wait()

    row_id = lax.broadcasted_iota(jnp.int32, (rows, dirs.shape[2]), 0)
    wave_id = lax.broadcasted_iota(jnp.int32, (rows, dirs.shape[2]), 1)
    chosen = wave_id == (H * c + q) * wl + row_id % wl

    def fill_weights(slot, xyz, qw):
        for a in range(halves):
            column = [
                (1.0 if a % 2 else 0.5)
                * jnp.sum(jnp.where(chosen, dirs[a, k : k + 1, :], 0.0), axis=1, keepdims=True)
                for k in range(3)
            ]
            for i in range(local // 128):
                lanes = pl.ds(i * 128, 128)
                w = qw[i : i + 1, :]
                weights[a, :, pl.ds(slot * local + i * 128, 128)] = (
                    column[0] * (xyz[0:1, lanes] * w)
                    + column[1] * (xyz[1:2, lanes] * w)
                    + column[2] * (xyz[2:3, lanes] * w)
                )

    fill_weights(0, coords, quad)
    for i in range(M // 128):
        lam[:, pl.ds(i * 128, 128)] = jnp.broadcast_to(rates[i : i + 1, :], (rows, 128))
    loads[-1].wait()

    pl.semaphore_wait(barrier, H * C + R + G - 1 + H - 1 - 2 * is_self.astype(jnp.int32))

    def first_copy(d, e):
        return pltpu.make_async_remote_copy(
            src_ref=start, dst_ref=landed.at[e, c], send_sem=first_send.at[d, e],
            recv_sem=first_recv.at[e, c], device_id=(H * (z ^ d) + (q ^ e), z),
            device_id_type=MESH,
        )

    for d in reversed(range(G)):
        for e in reversed(range(H)):
            unless(is_self & (d + e == 0), lambda d=d, e=e: first_copy(d, e).start())

    @pl.when(is_self)
    def _():
        pltpu.make_async_copy(start, landed.at[0, c], first_recv.at[0, c]).start()

    def to_core(e, src, dst, send, recv_sem):
        return pltpu.make_async_remote_copy(
            src_ref=src, dst_ref=dst, send_sem=send, recv_sem=recv_sem,
            device_id=(H * z + (q ^ e), c), device_id_type=MESH,
        )

    def geo_copy(e, which):
        src, dst = ((coords, coords_in), (quad, quad_in))[which]
        return to_core(
            e, src, dst.at[e - 1], geo_send.at[e - 1, which], geo_recv.at[e - 1, which]
        )

    def slab_copy(e, i):
        lanes = pl.ds(i * CHUNK, CHUNK)
        return to_core(
            e, basis.at[pl.ds(0, local), lanes], basis.at[pl.ds(e * local, local), lanes],
            slab_send.at[e - 1, i], slab_recv.at[e - 1, i],
        )

    def node_copy(e):
        return to_core(
            e, nodes_out.at[e - 1], nodes_in.at[e - 1], node_send.at[e - 1], node_recv.at[e - 1]
        )

    for e in range(1, H):
        for which in range(2):
            geo_copy(e, which).start()
    for i in range(chunks):
        for e in range(1, H):
            slab_copy(e, i).start()
    for e in range(1, H):
        for which in range(2):
            geo_copy(e, which).wait_recv()
        fill_weights(e, coords_in.at[e - 1], quad_in.at[e - 1])

    for e in reversed(range(H)):
        for s in range(C):
            pltpu.make_async_copy(start, landed.at[e, s], first_recv.at[e, s]).wait()
            for x in range(2):
                field[pl.ds(e * rows + x * wl, wl), pl.ds(s * width, width)] = landed[
                    e, s, x
                ].astype(jnp.float32)
    both[...] = field[...].astype(jnp.bfloat16)
    cur[...] = field[pl.ds(0, rows), :].astype(jnp.bfloat16)

    part_id = lax.broadcasted_iota(jnp.int32, (rows, local), 0) // wl

    def scale(total, a, slot):
        lanes = pl.ds(slot * local, local)
        v = total * weights[a, :, lanes]
        turned = jnp.where(part_id == 0, pltpu.roll(v, rows - wl, 0), -pltpu.roll(v, wl, 0))
        scaled[:, lanes] = turned.astype(jnp.bfloat16)

    total = lax.dot_general(
        both[...], basis[pl.ds(0, local), :], NT, preferred_element_type=jnp.float32
    )
    for e in range(1, H):
        nodes_out[e - 1] = total[e * rows : (e + 1) * rows, :]
        node_copy(e).start()
    scale(total[:rows, :], 0, 0)

    def part_copy(p, d, i):
        return pltpu.make_async_remote_copy(
            src_ref=parts.at[p, i], dst_ref=recv.at[p, d - 1, i],
            send_sem=part_send.at[p, d - 1, i], recv_sem=part_recv.at[p, d - 1, i],
            device_id=(H * (z ^ d) + q, c), device_id_type=MESH,
        )

    def send_part(p, i, block):
        parts[p, i] = block.astype(jnp.bfloat16)
        for d in reversed(range(1, G)):
            part_copy(p, d, i).start()

    def chunk_of(i):
        return pl.ds(i * CHUNK, CHUNK)

    for i in range(chunks):
        early[:, chunk_of(i)] = lax.dot_general(
            scaled[:, pl.ds(0, local)], basis[pl.ds(0, local), chunk_of(i)], NN,
            preferred_element_type=jnp.float32,
        )
    for e in range(1, H):
        node_copy(e).wait_recv()
        scale(nodes_in[e - 1], 0, e)
    for i in range(chunks):
        for e in range(1, H):
            slab_copy(e, i).wait_recv()
        send_part(0, i, early[:, chunk_of(i)] + lax.dot_general(
            scaled[:, pl.ds(local, (H - 1) * local)],
            basis[pl.ds(local, (H - 1) * local), chunk_of(i)], NN,
            preferred_element_type=jnp.float32,
        ))

    def finish(step):
        p = lax.rem(step, 2)
        odd = p == 1
        factor = jnp.where(odd, 1.0, 0.5).astype(jnp.float32)
        total = jnp.zeros((rows, H * local), jnp.float32)
        for i in range(chunks):
            lanes = chunk_of(i)
            old = field[pl.ds(0, rows), lanes]
            acc = old - (factor * lam[:, lanes]) * cur[:, lanes].astype(jnp.float32)
            acc = acc + parts[p, i].astype(jnp.float32)
            for d in range(1, G):
                part_copy(p, d, i).wait_recv()
                acc = acc + recv[p, d - 1, i].astype(jnp.float32)
            rounded = acc.astype(jnp.bfloat16)
            cur[:, lanes] = rounded
            field[pl.ds(0, rows), lanes] = jnp.where(odd, rounded.astype(jnp.float32), old)
            total = total + lax.dot_general(
                rounded, basis[:, lanes], NT, preferred_element_type=jnp.float32
            )
        for slot in range(H):
            scale(total[:, slot * local : (slot + 1) * local], step + 1, slot)

    def sent(p):
        for i in range(chunks):
            for d in range(1, G):
                part_copy(p, d, i).wait_send()

    def half_step(step, carry):
        finish(step)
        p = lax.rem(step, 2)
        v = scaled[...]
        for i in range(chunks):
            send_part(1 - p, i, lax.dot_general(
                v, basis[:, chunk_of(i)], NN, preferred_element_type=jnp.float32
            ))
        sent(p)
        return carry

    lax.fori_loop(0, halves - 2, half_step, 0)
    finish(halves - 2)

    def last_copy(d):
        return pltpu.make_async_remote_copy(
            src_ref=lastout.at[d], dst_ref=lastin.at[z], send_sem=last_send.at[d],
            recv_sem=last_recv.at[z], device_id=(H * c + q, c ^ d), device_id_type=MESH,
        )

    v = scaled[...]
    for d in reversed(range(C)):
        lanes = pl.ds(pl.multiple_of((c ^ d) * width, width), width)
        rest = field[pl.ds(0, rows), lanes] - lam[:, lanes] * cur[:, lanes].astype(jnp.float32)
        block = lax.dot_general(v, basis[:, lanes], NN, preferred_element_type=jnp.float32)
        lastout[d] = (block + jnp.where(is_self, rest, 0.0)).astype(jnp.bfloat16)
        if d:
            last_copy(d).start()
    unless(is_self, lambda: last_copy(0).start())

    @pl.when(is_self)
    def _():
        pltpu.make_async_copy(lastout.at[0], lastin.at[z], last_recv.at[z]).start()

    fresh = jnp.zeros((rows, width), jnp.float32)
    for s in range(G):
        pltpu.make_async_copy(lastout.at[0], lastin.at[s], last_recv.at[s]).wait()
        fresh = fresh + lastin[s].astype(jnp.float32)
    for x in range(2):
        out[x] = fresh[x * wl : (x + 1) * wl, :].astype(jnp.bfloat16)

    sent((halves - 2) % 2)
    for d in range(C):
        unless(is_self & (d == 0), lambda d=d: last_copy(d).wait_send())
    for d in range(G):
        for e in range(H):
            unless(is_self & (d + e == 0), lambda d=d, e=e: first_copy(d, e).wait_send())
    for e in range(1, H):
        node_copy(e).wait_send()
        for which in range(2):
            geo_copy(e, which).wait_send()
        for i in range(chunks):
            slab_copy(e, i).wait_send()


def on_device(R, C, basis, coords, quad, magnetization, rates, dirs):
    H = R // C
    G = R // H
    local, M = basis.shape
    start = jnp.transpose(magnetization, (0, 2, 1))
    quad = quad.reshape(-1, 128)
    rates = rates.reshape(-1, 128)
    _, wl, width = start.shape
    rows = 2 * wl
    chunks = M // CHUNK
    dma = pltpu.SemaphoreType.DMA
    bf16, f32 = jnp.bfloat16, jnp.float32
    result = pl.pallas_call(
        functools.partial(kernel, R, C),
        out_shape=jax.ShapeDtypeStruct(start.shape, bf16),
        in_specs=[pl.BlockSpec(memory_space=pl.ANY)] * 6,
        out_specs=pl.BlockSpec(memory_space=pltpu.VMEM),
        scratch_shapes=[
            pltpu.VMEM((H * local, M), bf16),
            pltpu.VMEM(coords.shape, f32),
            pltpu.VMEM(quad.shape, f32),
            pltpu.VMEM(rates.shape, f32),
            pltpu.VMEM(dirs.shape, f32),
            pltpu.VMEM((H, C, 2, wl, width), bf16),
            pltpu.VMEM((rows, M), bf16),
            pltpu.VMEM((H * rows, M), f32),
            pltpu.VMEM((H * rows, M), bf16),
            pltpu.VMEM((rows, M), f32),
            pltpu.VMEM((rows, M), f32),
            pltpu.VMEM((2, chunks, rows, CHUNK), bf16),
            pltpu.VMEM((2, G - 1, chunks, rows, CHUNK), bf16),
            pltpu.VMEM((2 * STEPS, rows, H * local), f32),
            pltpu.VMEM((H - 1,) + coords.shape, f32),
            pltpu.VMEM((H - 1,) + quad.shape, f32),
            pltpu.VMEM((H - 1, rows, local), f32),
            pltpu.VMEM((H - 1, rows, local), f32),
            pltpu.VMEM((rows, H * local), bf16),
            pltpu.VMEM((C, rows, width), bf16),
            pltpu.VMEM((G, rows, width), bf16),
            dma((5,)),
            dma((H - 1, chunks)), dma((H - 1, chunks)),
            dma((H - 1, 2)), dma((H - 1, 2)),
            dma((G, H)), dma((H, C)),
            dma((H - 1,)), dma((H - 1,)),
            dma((2, G - 1, chunks)), dma((2, G - 1, chunks)),
            dma((C,)), dma((G,)),
        ],
        compiler_params=pltpu.CompilerParams(collective_id=0, has_side_effects=True),
    )(basis, coords, quad, start, rates, dirs)
    return jnp.transpose(result, (0, 2, 1))


def solution(mesh):
    return jax.shard_map(
        functools.partial(on_device, mesh.shape["row"], mesh.shape["col"]),
        mesh=mesh,
        in_specs=(P("row", None), P(None, "row"), P("row"), P(None, "col", "row"), P(), P()),
        out_specs=P(None, "col", "row"),
        check_vma=False,
    )
```

```python
import functools

import jax
import jax.numpy as jnp
from jax import lax
from jax.experimental import pallas as pl
from jax.experimental.pallas import tpu as pltpu
from jax.sharding import PartitionSpec as P

STEPS = 3
CHUNKS = (512,) * 8
MESH = pl.DeviceIdType.MESH
NT = (((1,), (1,)), ((), ()))
NN = (((1,), (0,)), ((), ()))


def cuts_of(M):
    starts = [sum(CHUNKS[:i]) for i in range(len(CHUNKS))]
    return list(zip(starts, CHUNKS))


def kernel(
    R, C, basis_hbm, coords_hbm, quad_hbm, start, rates_hbm, dirs_hbm, out,
    basis, coords, quad, rates, dirs, landed, cur, field, ready, lam, early, parts, recv, weights,
    coords_in, quad_in, nodes_out, nodes_in, scaled, lastout, lastin,
    load_sem, slab_send, slab_recv, geo_send, geo_recv, first_send, first_recv,
    node_send, node_recv, part_send, part_recv, last_send, last_recv,
):
    H = R // C
    G = R // H
    r = lax.axis_index("row")
    c = lax.axis_index("col")
    z = r // H
    q = lax.rem(r, H)
    wl, width = start.shape[1], start.shape[2]
    rows = 2 * wl
    local = basis_hbm.shape[0]
    M = basis_hbm.shape[1]
    halves = 2 * STEPS
    cuts = cuts_of(M)
    chunks = len(cuts)

    barrier = pltpu.get_barrier_semaphore()
    is_self = z == c

    def greet(row, col):
        pl.semaphore_signal(barrier, inc=1, device_id=(row, col), device_id_type=MESH)

    def unless(cond, fn):
        pl.when(jnp.logical_not(cond))(fn)

    for d in reversed(range(C)):
        for e in range(H):
            unless(is_self & (d + e == 0), functools.partial(greet, H * c + (q ^ e), c ^ d))
    for d in reversed(range(G)):
        for e in range(H):
            unless(is_self & (d + e == 0), functools.partial(greet, H * (z ^ d) + (q ^ e), z))
    for d in range(1, G):
        greet(H * (z ^ d) + q, c)
    for e in range(1, H):
        greet(H * z + (q ^ e), c)

    loads = [
        pltpu.make_async_copy(src, dst, load_sem.at[k])
        for k, (src, dst) in enumerate((
            (coords_hbm, coords), (quad_hbm, quad), (rates_hbm, rates), (dirs_hbm, dirs),
            (basis_hbm, basis.at[pl.ds(0, local), :]),
        ))
    ]
    for load in loads:
        load.start()
    for load in loads[:-1]:
        load.wait()

    row_id = lax.broadcasted_iota(jnp.int32, (rows, dirs.shape[2]), 0)
    wave_id = lax.broadcasted_iota(jnp.int32, (rows, dirs.shape[2]), 1)
    chosen = wave_id == (H * c + q) * wl + row_id % wl

    def fill_weights(slot, xyz, qw):
        for a in range(halves):
            column = [
                (1.0 if a % 2 else 0.5)
                * jnp.sum(jnp.where(chosen, dirs[a, k : k + 1, :], 0.0), axis=1, keepdims=True)
                for k in range(3)
            ]
            for i in range(local // 128):
                lanes = pl.ds(i * 128, 128)
                w = qw[i : i + 1, :]
                weights[a, :, pl.ds(slot * local + i * 128, 128)] = (
                    column[0] * (xyz[0:1, lanes] * w)
                    + column[1] * (xyz[1:2, lanes] * w)
                    + column[2] * (xyz[2:3, lanes] * w)
                )

    fill_weights(0, coords, quad)
    for i in range(M // 128):
        lam[:, pl.ds(i * 128, 128)] = jnp.broadcast_to(rates[i : i + 1, :], (rows, 128))
    loads[-1].wait()

    pl.semaphore_wait(barrier, H * C + R + G - 1 + H - 1 - 2 * is_self.astype(jnp.int32))

    def first_copy(d, e):
        return pltpu.make_async_remote_copy(
            src_ref=start, dst_ref=landed.at[e, c], send_sem=first_send.at[d, e],
            recv_sem=first_recv.at[e, c], device_id=(H * (z ^ d) + (q ^ e), z),
            device_id_type=MESH,
        )

    for d in reversed(range(G)):
        for e in reversed(range(H)):
            unless(is_self & (d + e == 0), lambda d=d, e=e: first_copy(d, e).start())

    @pl.when(is_self)
    def _():
        pltpu.make_async_copy(start, landed.at[0, c], first_recv.at[0, c]).start()

    def to_core(e, src, dst, send, recv_sem):
        return pltpu.make_async_remote_copy(
            src_ref=src, dst_ref=dst, send_sem=send, recv_sem=recv_sem,
            device_id=(H * z + (q ^ e), c), device_id_type=MESH,
        )

    def geo_copy(e, which):
        src, dst = ((coords, coords_in), (quad, quad_in))[which]
        return to_core(
            e, src, dst.at[e - 1], geo_send.at[e - 1, which], geo_recv.at[e - 1, which]
        )

    def chunk_of(i):
        return pl.ds(*cuts[i])

    def slab_copy(e, i):
        lanes = chunk_of(i)
        return to_core(
            e, basis.at[pl.ds(0, local), lanes], basis.at[pl.ds(e * local, local), lanes],
            slab_send.at[e - 1, i], slab_recv.at[e - 1, i],
        )

    def node_copy(e):
        return to_core(
            e, nodes_out.at[e - 1], nodes_in.at[e - 1], node_send.at[e - 1], node_recv.at[e - 1]
        )

    for e in range(1, H):
        for which in range(2):
            geo_copy(e, which).start()
    for i in range(chunks):
        for e in range(1, H):
            slab_copy(e, i).start()
    for e in range(1, H):
        for which in range(2):
            geo_copy(e, which).wait_recv()
        fill_weights(e, coords_in.at[e - 1], quad_in.at[e - 1])

    part_id = lax.broadcasted_iota(jnp.int32, (rows, local), 0) // wl

    def scale(total, a, slot):
        lanes = pl.ds(slot * local, local)
        v = total * weights[a, :, lanes]
        turned = jnp.where(part_id == 0, pltpu.roll(v, rows - wl, 0), -pltpu.roll(v, wl, 0))
        scaled[:, lanes] = turned.astype(jnp.bfloat16)

    total = jnp.zeros((H * rows, local), jnp.float32)
    for d in range(C):
        s = c ^ d
        lanes = pl.ds(pl.multiple_of(s * width, width), width)
        for e in range(H):
            pltpu.make_async_copy(start, landed.at[e, s], first_recv.at[e, s]).wait()
            for x in range(2):
                field[pl.ds(e * rows + x * wl, wl), lanes] = landed[e, s, x].astype(jnp.float32)
        block = field[:, lanes].astype(jnp.bfloat16)
        cur[:, lanes] = block[:rows, :]
        total = total + lax.dot_general(
            block, basis[pl.ds(0, local), lanes], NT, preferred_element_type=jnp.float32
        )
    for e in range(1, H):
        nodes_out[e - 1] = total[e * rows : (e + 1) * rows, :]
        node_copy(e).start()
    scale(total[:rows, :], 0, 0)

    def part_copy(p, d, i):
        return pltpu.make_async_remote_copy(
            src_ref=parts.at[p, :, chunk_of(i)], dst_ref=recv.at[p, d - 1, :, chunk_of(i)],
            send_sem=part_send.at[p, d - 1, i], recv_sem=part_recv.at[p, d - 1, i],
            device_id=(H * (z ^ d) + q, c), device_id_type=MESH,
        )

    def send_part(p, i, block):
        parts[p, :, chunk_of(i)] = block.astype(jnp.bfloat16)
        for d in reversed(range(1, G)):
            part_copy(p, d, i).start()

    for i in range(chunks):
        early[:, chunk_of(i)] = lax.dot_general(
            scaled[:, pl.ds(0, local)], basis[pl.ds(0, local), chunk_of(i)], NN,
            preferred_element_type=jnp.float32,
        )
    for e in range(1, H):
        node_copy(e).wait_recv()
        scale(nodes_in[e - 1], 0, e)
    for i in range(chunks):
        for e in range(1, H):
            slab_copy(e, i).wait_recv()
        send_part(0, i, early[:, chunk_of(i)] + lax.dot_general(
            scaled[:, pl.ds(local, (H - 1) * local)],
            basis[pl.ds(local, (H - 1) * local), chunk_of(i)], NN,
            preferred_element_type=jnp.float32,
        ))

    def finish(step):
        p = lax.rem(step, 2)
        odd = p == 1
        factor = jnp.where(odd, 1.0, 0.5).astype(jnp.float32)
        for i in range(chunks):
            lanes = chunk_of(i)
            ready[:, lanes] = (
                field[pl.ds(0, rows), lanes]
                - (factor * lam[:, lanes]) * cur[:, lanes].astype(jnp.float32)
                + parts[p, :, lanes].astype(jnp.float32)
            )
        total = jnp.zeros((rows, H * local), jnp.float32)
        for i in range(chunks):
            lanes = chunk_of(i)
            acc = ready[:, lanes]
            for d in range(1, G):
                part_copy(p, d, i).wait_recv()
                acc = acc + recv[p, d - 1, :, lanes].astype(jnp.float32)
            rounded = acc.astype(jnp.bfloat16)
            cur[:, lanes] = rounded
            field[pl.ds(0, rows), lanes] = jnp.where(
                odd, rounded.astype(jnp.float32), field[pl.ds(0, rows), lanes]
            )
            total = total + lax.dot_general(
                rounded, basis[:, lanes], NT, preferred_element_type=jnp.float32
            )
        for slot in range(H):
            scale(total[:, slot * local : (slot + 1) * local], step + 1, slot)

    def sent(p):
        for i in range(chunks):
            for d in range(1, G):
                part_copy(p, d, i).wait_send()

    def half_step(step, carry):
        finish(step)
        p = lax.rem(step, 2)
        v = scaled[...]
        for i in range(chunks):
            send_part(1 - p, i, lax.dot_general(
                v, basis[:, chunk_of(i)], NN, preferred_element_type=jnp.float32
            ))
        sent(p)
        return carry

    lax.fori_loop(0, halves - 2, half_step, 0)
    finish(halves - 2)

    def last_copy(d):
        return pltpu.make_async_remote_copy(
            src_ref=lastout.at[d], dst_ref=lastin.at[z], send_sem=last_send.at[d],
            recv_sem=last_recv.at[z], device_id=(H * c + q, c ^ d), device_id_type=MESH,
        )

    v = scaled[...]
    for d in reversed(range(C)):
        lanes = pl.ds(pl.multiple_of((c ^ d) * width, width), width)
        rest = field[pl.ds(0, rows), lanes] - lam[:, lanes] * cur[:, lanes].astype(jnp.float32)
        block = lax.dot_general(v, basis[:, lanes], NN, preferred_element_type=jnp.float32)
        lastout[d] = (block + jnp.where(is_self, rest, 0.0)).astype(jnp.bfloat16)
        if d:
            last_copy(d).start()
    unless(is_self, lambda: last_copy(0).start())

    @pl.when(is_self)
    def _():
        pltpu.make_async_copy(lastout.at[0], lastin.at[z], last_recv.at[z]).start()

    fresh = jnp.zeros((rows, width), jnp.float32)
    for s in range(G):
        pltpu.make_async_copy(lastout.at[0], lastin.at[s], last_recv.at[s]).wait()
        fresh = fresh + lastin[s].astype(jnp.float32)
    for x in range(2):
        out[x] = fresh[x * wl : (x + 1) * wl, :].astype(jnp.bfloat16)

    sent((halves - 2) % 2)
    for d in range(C):
        unless(is_self & (d == 0), lambda d=d: last_copy(d).wait_send())
    for d in range(G):
        for e in range(H):
            unless(is_self & (d + e == 0), lambda d=d, e=e: first_copy(d, e).wait_send())
    for e in range(1, H):
        node_copy(e).wait_send()
        for which in range(2):
            geo_copy(e, which).wait_send()
        for i in range(chunks):
            slab_copy(e, i).wait_send()


def on_device(R, C, basis, coords, quad, magnetization, rates, dirs):
    H = R // C
    G = R // H
    local, M = basis.shape
    start = jnp.transpose(magnetization, (0, 2, 1))
    quad = quad.reshape(-1, 128)
    rates = rates.reshape(-1, 128)
    _, wl, width = start.shape
    rows = 2 * wl
    cuts = cuts_of(M)
    chunks = len(cuts)
    dma = pltpu.SemaphoreType.DMA
    bf16, f32 = jnp.bfloat16, jnp.float32
    result = pl.pallas_call(
        functools.partial(kernel, R, C),
        out_shape=pltpu.VMEM(start.shape, bf16),
        in_specs=[pl.BlockSpec(memory_space=pl.ANY)] * 6,
        out_specs=pl.BlockSpec(memory_space=pltpu.VMEM),
        scratch_shapes=[
            pltpu.VMEM((H * local, M), bf16),
            pltpu.VMEM(coords.shape, f32),
            pltpu.VMEM(quad.shape, f32),
            pltpu.VMEM(rates.shape, f32),
            pltpu.VMEM(dirs.shape, f32),
            pltpu.VMEM((H, C, 2, wl, width), bf16),
            pltpu.VMEM((rows, M), bf16),
            pltpu.VMEM((H * rows, M), f32),
            pltpu.VMEM((rows, M), f32),
            pltpu.VMEM((rows, M), f32),
            pltpu.VMEM((rows, M), f32),
            pltpu.VMEM((2, rows, M), bf16),
            pltpu.VMEM((2, G - 1, rows, M), bf16),
            pltpu.VMEM((2 * STEPS, rows, H * local), f32),
            pltpu.VMEM((H - 1,) + coords.shape, f32),
            pltpu.VMEM((H - 1,) + quad.shape, f32),
            pltpu.VMEM((H - 1, rows, local), f32),
            pltpu.VMEM((H - 1, rows, local), f32),
            pltpu.VMEM((rows, H * local), bf16),
            pltpu.VMEM((C, rows, width), bf16),
            pltpu.VMEM((G, rows, width), bf16),
            dma((5,)),
            dma((H - 1, chunks)), dma((H - 1, chunks)),
            dma((H - 1, 2)), dma((H - 1, 2)),
            dma((G, H)), dma((H, C)),
            dma((H - 1,)), dma((H - 1,)),
            dma((2, G - 1, chunks)), dma((2, G - 1, chunks)),
            dma((C,)), dma((G,)),
        ],
        compiler_params=pltpu.CompilerParams(collective_id=0, has_side_effects=True),
    )(basis, coords, quad, start, rates, dirs)
    return jnp.transpose(result, (0, 2, 1))


def solution(mesh):
    return jax.shard_map(
        functools.partial(on_device, mesh.shape["row"], mesh.shape["col"]),
        mesh=mesh,
        in_specs=(P("row", None), P(None, "row"), P("row"), P(None, "col", "row"), P(), P()),
        out_specs=P(None, "col", "row"),
        check_vma=False,
    )
```

```python
import functools

import jax
import jax.numpy as jnp
from jax import lax
from jax.experimental import pallas as pl
from jax.experimental.pallas import tpu as pltpu
from jax.sharding import PartitionSpec as P

STEPS = 3
CHUNKS = (512,) * 8
MESH = pl.DeviceIdType.MESH
NT = (((1,), (1,)), ((), ()))
NN = (((1,), (0,)), ((), ()))


def cuts_of(M):
    starts = [sum(CHUNKS[:i]) for i in range(len(CHUNKS))]
    return list(zip(starts, CHUNKS))


def kernel(
    R, C, basis_hbm, coords_hbm, quad_hbm, start, rates_hbm, dirs_hbm, out,
    basis, coords, quad, rates, dirs, landed, cur, field, ready, lam, early, parts, recv, weights,
    coords_in, quad_in, nodes_out, nodes_in, scaled, lastout, lastin,
    load_sem, slab_send, slab_recv, geo_send, geo_recv, first_send, first_recv,
    node_send, node_recv, part_send, part_recv, last_send, last_recv,
):
    H = R // C
    G = R // H
    r = lax.axis_index("row")
    c = lax.axis_index("col")
    z = r // H
    q = lax.rem(r, H)
    wl, width = start.shape[1], start.shape[2]
    rows = 2 * wl
    local = basis_hbm.shape[0]
    M = basis_hbm.shape[1]
    halves = 2 * STEPS
    cuts = cuts_of(M)
    chunks = len(cuts)

    barrier = pltpu.get_barrier_semaphore()
    is_self = z == c

    def greet(row, col):
        pl.semaphore_signal(barrier, inc=1, device_id=(row, col), device_id_type=MESH)

    def unless(cond, fn):
        pl.when(jnp.logical_not(cond))(fn)

    for d in reversed(range(C)):
        for e in range(H):
            unless(is_self & (d + e == 0), functools.partial(greet, H * c + (q ^ e), c ^ d))
    for d in reversed(range(G)):
        for e in range(H):
            unless(is_self & (d + e == 0), functools.partial(greet, H * (z ^ d) + (q ^ e), z))
    for d in range(1, G):
        greet(H * (z ^ d) + q, c)
    for e in range(1, H):
        greet(H * z + (q ^ e), c)

    loads = [
        pltpu.make_async_copy(src, dst, load_sem.at[k])
        for k, (src, dst) in enumerate((
            (coords_hbm, coords), (quad_hbm, quad), (rates_hbm, rates), (dirs_hbm, dirs),
            (basis_hbm, basis.at[pl.ds(0, local), :]),
        ))
    ]
    for load in loads:
        load.start()
    for load in loads[:-1]:
        load.wait()

    row_id = lax.broadcasted_iota(jnp.int32, (rows, dirs.shape[2]), 0)
    wave_id = lax.broadcasted_iota(jnp.int32, (rows, dirs.shape[2]), 1)
    chosen = wave_id == (H * c + q) * wl + row_id % wl

    def fill_weights(slot, xyz, qw):
        for a in range(halves):
            column = [
                (1.0 if a % 2 else 0.5)
                * jnp.sum(jnp.where(chosen, dirs[a, k : k + 1, :], 0.0), axis=1, keepdims=True)
                for k in range(3)
            ]
            for i in range(local // 128):
                lanes = pl.ds(i * 128, 128)
                w = qw[i : i + 1, :]
                weights[a, :, pl.ds(slot * local + i * 128, 128)] = (
                    column[0] * (xyz[0:1, lanes] * w)
                    + column[1] * (xyz[1:2, lanes] * w)
                    + column[2] * (xyz[2:3, lanes] * w)
                )

    fill_weights(0, coords, quad)
    for i in range(M // 128):
        lam[:, pl.ds(i * 128, 128)] = jnp.broadcast_to(rates[i : i + 1, :], (rows, 128))
    loads[-1].wait()

    pl.semaphore_wait(barrier, H * C + R + G - 1 + H - 1 - 2 * is_self.astype(jnp.int32))

    def first_copy(d, e):
        return pltpu.make_async_remote_copy(
            src_ref=start, dst_ref=landed.at[e, c], send_sem=first_send.at[d, e],
            recv_sem=first_recv.at[e, c], device_id=(H * (z ^ d) + (q ^ e), z),
            device_id_type=MESH,
        )

    for d in reversed(range(G)):
        for e in reversed(range(H)):
            unless(is_self & (d + e == 0), lambda d=d, e=e: first_copy(d, e).start())

    @pl.when(is_self)
    def _():
        pltpu.make_async_copy(start, landed.at[0, c], first_recv.at[0, c]).start()

    def to_core(e, src, dst, send, recv_sem):
        return pltpu.make_async_remote_copy(
            src_ref=src, dst_ref=dst, send_sem=send, recv_sem=recv_sem,
            device_id=(H * z + (q ^ e), c), device_id_type=MESH,
        )

    def geo_copy(e, which):
        src, dst = ((coords, coords_in), (quad, quad_in))[which]
        return to_core(
            e, src, dst.at[e - 1], geo_send.at[e - 1, which], geo_recv.at[e - 1, which]
        )

    def chunk_of(i):
        return pl.ds(*cuts[i])

    def slab_copy(e, i):
        lanes = chunk_of(i)
        return to_core(
            e, basis.at[pl.ds(0, local), lanes], basis.at[pl.ds(e * local, local), lanes],
            slab_send.at[e - 1, i], slab_recv.at[e - 1, i],
        )

    def node_copy(e):
        return to_core(
            e, nodes_out.at[e - 1], nodes_in.at[e - 1], node_send.at[e - 1], node_recv.at[e - 1]
        )

    for e in range(1, H):
        for which in range(2):
            geo_copy(e, which).start()
    for i in range(chunks):
        for e in range(1, H):
            slab_copy(e, i).start()
    for e in range(1, H):
        for which in range(2):
            geo_copy(e, which).wait_recv()
        fill_weights(e, coords_in.at[e - 1], quad_in.at[e - 1])

    part_id = lax.broadcasted_iota(jnp.int32, (rows, local), 0) // wl

    def scale(total, a, slot):
        lanes = pl.ds(slot * local, local)
        v = total * weights[a, :, lanes]
        turned = jnp.where(part_id == 0, pltpu.roll(v, rows - wl, 0), -pltpu.roll(v, wl, 0))
        scaled[:, lanes] = turned.astype(jnp.bfloat16)

    total = jnp.zeros((H * rows, local), jnp.float32)
    for d in range(C):
        s = c ^ d
        lanes = pl.ds(pl.multiple_of(s * width, width), width)
        for e in range(H):
            pltpu.make_async_copy(start, landed.at[e, s], first_recv.at[e, s]).wait()
            for x in range(2):
                field[pl.ds(e * rows + x * wl, wl), lanes] = landed[e, s, x].astype(jnp.float32)
        block = field[:, lanes].astype(jnp.bfloat16)
        cur[:, lanes] = block[:rows, :]
        total = total + lax.dot_general(
            block, basis[pl.ds(0, local), lanes], NT, preferred_element_type=jnp.float32
        )
    for e in range(1, H):
        nodes_out[e - 1] = total[e * rows : (e + 1) * rows, :]
        node_copy(e).start()
    scale(total[:rows, :], 0, 0)

    def part_copy(p, d, i):
        return pltpu.make_async_remote_copy(
            src_ref=parts.at[p, :, chunk_of(i)], dst_ref=recv.at[p, d - 1, :, chunk_of(i)],
            send_sem=part_send.at[p, d - 1, i], recv_sem=part_recv.at[p, d - 1, i],
            device_id=(H * (z ^ d) + q, c), device_id_type=MESH,
        )

    def send_part(p, i, block):
        parts[p, :, chunk_of(i)] = block.astype(jnp.bfloat16)
        for d in [d for d in reversed(range(1, G)) if d != 2] + [2]:
            part_copy(p, d, i).start()

    for i in range(chunks):
        early[:, chunk_of(i)] = lax.dot_general(
            scaled[:, pl.ds(0, local)], basis[pl.ds(0, local), chunk_of(i)], NN,
            preferred_element_type=jnp.float32,
        )
    for e in range(1, H):
        node_copy(e).wait_recv()
        scale(nodes_in[e - 1], 0, e)
    for i in range(chunks):
        for e in range(1, H):
            slab_copy(e, i).wait_recv()
        send_part(0, i, early[:, chunk_of(i)] + lax.dot_general(
            scaled[:, pl.ds(local, (H - 1) * local)],
            basis[pl.ds(local, (H - 1) * local), chunk_of(i)], NN,
            preferred_element_type=jnp.float32,
        ))

    def finish(step):
        p = lax.rem(step, 2)
        odd = p == 1
        factor = jnp.where(odd, 1.0, 0.5).astype(jnp.float32)
        for i in range(chunks):
            lanes = chunk_of(i)
            ready[:, lanes] = (
                field[pl.ds(0, rows), lanes]
                - (factor * lam[:, lanes]) * cur[:, lanes].astype(jnp.float32)
                + parts[p, :, lanes].astype(jnp.float32)
            )
        total = jnp.zeros((rows, H * local), jnp.float32)
        for i in range(chunks):
            lanes = chunk_of(i)
            acc = ready[:, lanes]
            for d in range(1, G):
                part_copy(p, d, i).wait_recv()
                acc = acc + recv[p, d - 1, :, lanes].astype(jnp.float32)
            rounded = acc.astype(jnp.bfloat16)
            cur[:, lanes] = rounded
            field[pl.ds(0, rows), lanes] = jnp.where(
                odd, rounded.astype(jnp.float32), field[pl.ds(0, rows), lanes]
            )
            total = total + lax.dot_general(
                rounded, basis[:, lanes], NT, preferred_element_type=jnp.float32
            )
        for slot in range(H):
            scale(total[:, slot * local : (slot + 1) * local], step + 1, slot)

    def sent(p):
        for i in range(chunks):
            for d in range(1, G):
                part_copy(p, d, i).wait_send()

    def half_step(step, carry):
        finish(step)
        p = lax.rem(step, 2)
        v = scaled[...]
        for i in range(chunks):
            send_part(1 - p, i, lax.dot_general(
                v, basis[:, chunk_of(i)], NN, preferred_element_type=jnp.float32
            ))
        sent(p)
        return carry

    lax.fori_loop(0, halves - 2, half_step, 0)
    finish(halves - 2)

    def last_copy(d):
        return pltpu.make_async_remote_copy(
            src_ref=lastout.at[d], dst_ref=lastin.at[z], send_sem=last_send.at[d],
            recv_sem=last_recv.at[z], device_id=(H * c + q, c ^ d), device_id_type=MESH,
        )

    v = scaled[...]
    for d in reversed(range(C)):
        lanes = pl.ds(pl.multiple_of((c ^ d) * width, width), width)
        rest = field[pl.ds(0, rows), lanes] - lam[:, lanes] * cur[:, lanes].astype(jnp.float32)
        block = lax.dot_general(v, basis[:, lanes], NN, preferred_element_type=jnp.float32)
        lastout[d] = (block + jnp.where(is_self, rest, 0.0)).astype(jnp.bfloat16)
        if d:
            last_copy(d).start()
    unless(is_self, lambda: last_copy(0).start())

    @pl.when(is_self)
    def _():
        pltpu.make_async_copy(lastout.at[0], lastin.at[z], last_recv.at[z]).start()

    fresh = jnp.zeros((rows, width), jnp.float32)
    for s in range(G):
        pltpu.make_async_copy(lastout.at[0], lastin.at[s], last_recv.at[s]).wait()
        fresh = fresh + lastin[s].astype(jnp.float32)
    for x in range(2):
        out[x] = fresh[x * wl : (x + 1) * wl, :].astype(jnp.bfloat16)

    sent((halves - 2) % 2)
    for d in range(C):
        unless(is_self & (d == 0), lambda d=d: last_copy(d).wait_send())
    for d in range(G):
        for e in range(H):
            unless(is_self & (d + e == 0), lambda d=d, e=e: first_copy(d, e).wait_send())
    for e in range(1, H):
        node_copy(e).wait_send()
        for which in range(2):
            geo_copy(e, which).wait_send()
        for i in range(chunks):
            slab_copy(e, i).wait_send()


def on_device(R, C, basis, coords, quad, magnetization, rates, dirs):
    H = R // C
    G = R // H
    local, M = basis.shape
    start = jnp.transpose(magnetization, (0, 2, 1))
    quad = quad.reshape(-1, 128)
    rates = rates.reshape(-1, 128)
    _, wl, width = start.shape
    rows = 2 * wl
    cuts = cuts_of(M)
    chunks = len(cuts)
    dma = pltpu.SemaphoreType.DMA
    bf16, f32 = jnp.bfloat16, jnp.float32
    result = pl.pallas_call(
        functools.partial(kernel, R, C),
        out_shape=pltpu.VMEM(start.shape, bf16),
        in_specs=[pl.BlockSpec(memory_space=pl.ANY)] * 6,
        out_specs=pl.BlockSpec(memory_space=pltpu.VMEM),
        scratch_shapes=[
            pltpu.VMEM((H * local, M), bf16),
            pltpu.VMEM(coords.shape, f32),
            pltpu.VMEM(quad.shape, f32),
            pltpu.VMEM(rates.shape, f32),
            pltpu.VMEM(dirs.shape, f32),
            pltpu.VMEM((H, C, 2, wl, width), bf16),
            pltpu.VMEM((rows, M), bf16),
            pltpu.VMEM((H * rows, M), f32),
            pltpu.VMEM((rows, M), f32),
            pltpu.VMEM((rows, M), f32),
            pltpu.VMEM((rows, M), f32),
            pltpu.VMEM((2, rows, M), bf16),
            pltpu.VMEM((2, G - 1, rows, M), bf16),
            pltpu.VMEM((2 * STEPS, rows, H * local), f32),
            pltpu.VMEM((H - 1,) + coords.shape, f32),
            pltpu.VMEM((H - 1,) + quad.shape, f32),
            pltpu.VMEM((H - 1, rows, local), f32),
            pltpu.VMEM((H - 1, rows, local), f32),
            pltpu.VMEM((rows, H * local), bf16),
            pltpu.VMEM((C, rows, width), bf16),
            pltpu.VMEM((G, rows, width), bf16),
            dma((5,)),
            dma((H - 1, chunks)), dma((H - 1, chunks)),
            dma((H - 1, 2)), dma((H - 1, 2)),
            dma((G, H)), dma((H, C)),
            dma((H - 1,)), dma((H - 1,)),
            dma((2, G - 1, chunks)), dma((2, G - 1, chunks)),
            dma((C,)), dma((G,)),
        ],
        compiler_params=pltpu.CompilerParams(collective_id=0, has_side_effects=True),
    )(basis, coords, quad, start, rates, dirs)
    return jnp.transpose(result, (0, 2, 1))


def solution(mesh):
    return jax.shard_map(
        functools.partial(on_device, mesh.shape["row"], mesh.shape["col"]),
        mesh=mesh,
        in_specs=(P("row", None), P(None, "row"), P("row"), P(None, "col", "row"), P(), P()),
        out_specs=P(None, "col", "row"),
        check_vma=False,
    )
```

```python
import functools

import jax
import jax.numpy as jnp
from jax import lax
from jax.experimental import pallas as pl
from jax.experimental.pallas import tpu as pltpu
from jax.sharding import PartitionSpec as P

STEPS = 3
CHUNKS = (512,) * 8
MESH = pl.DeviceIdType.MESH
NT = (((1,), (1,)), ((), ()))
NN = (((1,), (0,)), ((), ()))


def cuts_of(M):
    starts = [sum(CHUNKS[:i]) for i in range(len(CHUNKS))]
    return list(zip(starts, CHUNKS))


def kernel(
    R, C, basis_hbm, coords_hbm, quad_hbm, start, rates_hbm, dirs_hbm, out,
    basis, coords, quad, rates, dirs, landed, cur, field, ready, lam, early, parts, recv, weights,
    coords_in, quad_in, nodes_out, nodes_in, scaled, lastout, lastin,
    load_sem, slab_send, slab_recv, geo_send, geo_recv, first_send, first_recv,
    node_send, node_recv, turn, part_send, part_recv, last_send, last_recv,
):
    H = R // C
    G = R // H
    r = lax.axis_index("row")
    c = lax.axis_index("col")
    z = r // H
    q = lax.rem(r, H)
    wl, width = start.shape[1], start.shape[2]
    rows = 2 * wl
    local = basis_hbm.shape[0]
    M = basis_hbm.shape[1]
    halves = 2 * STEPS
    cuts = cuts_of(M)
    chunks = len(cuts)

    barrier = pltpu.get_barrier_semaphore()
    is_self = z == c

    def greet(row, col):
        pl.semaphore_signal(barrier, inc=1, device_id=(row, col), device_id_type=MESH)

    def unless(cond, fn):
        pl.when(jnp.logical_not(cond))(fn)

    for d in reversed(range(C)):
        for e in range(H):
            unless(is_self & (d + e == 0), functools.partial(greet, H * c + (q ^ e), c ^ d))
    for d in reversed(range(G)):
        for e in range(H):
            unless(is_self & (d + e == 0), functools.partial(greet, H * (z ^ d) + (q ^ e), z))
    for d in range(1, G):
        greet(H * (z ^ d) + q, c)
    for e in range(1, H):
        greet(H * z + (q ^ e), c)

    loads = [
        pltpu.make_async_copy(src, dst, load_sem.at[k])
        for k, (src, dst) in enumerate((
            (coords_hbm, coords), (quad_hbm, quad), (rates_hbm, rates), (dirs_hbm, dirs),
            (basis_hbm, basis.at[pl.ds(0, local), :]),
        ))
    ]
    for load in loads:
        load.start()
    for load in loads[:-1]:
        load.wait()

    row_id = lax.broadcasted_iota(jnp.int32, (rows, dirs.shape[2]), 0)
    wave_id = lax.broadcasted_iota(jnp.int32, (rows, dirs.shape[2]), 1)
    chosen = wave_id == (H * c + q) * wl + row_id % wl

    def fill_weights(slot, xyz, qw):
        for a in range(halves):
            column = [
                (1.0 if a % 2 else 0.5)
                * jnp.sum(jnp.where(chosen, dirs[a, k : k + 1, :], 0.0), axis=1, keepdims=True)
                for k in range(3)
            ]
            for i in range(local // 128):
                lanes = pl.ds(i * 128, 128)
                w = qw[i : i + 1, :]
                weights[a, :, pl.ds(slot * local + i * 128, 128)] = (
                    column[0] * (xyz[0:1, lanes] * w)
                    + column[1] * (xyz[1:2, lanes] * w)
                    + column[2] * (xyz[2:3, lanes] * w)
                )

    fill_weights(0, coords, quad)
    for i in range(M // 128):
        lam[:, pl.ds(i * 128, 128)] = jnp.broadcast_to(rates[i : i + 1, :], (rows, 128))
    loads[-1].wait()

    pl.semaphore_wait(barrier, H * C + R + G - 1 + H - 1 - 2 * is_self.astype(jnp.int32))

    def first_copy(d, e):
        return pltpu.make_async_remote_copy(
            src_ref=start, dst_ref=landed.at[e, c], send_sem=first_send.at[d, e],
            recv_sem=first_recv.at[e, c], device_id=(H * (z ^ d) + (q ^ e), z),
            device_id_type=MESH,
        )

    for d in reversed(range(G)):
        for e in reversed(range(H)):
            unless(is_self & (d + e == 0), lambda d=d, e=e: first_copy(d, e).start())

    @pl.when(is_self)
    def _():
        pltpu.make_async_copy(start, landed.at[0, c], first_recv.at[0, c]).start()

    def to_core(e, src, dst, send, recv_sem):
        return pltpu.make_async_remote_copy(
            src_ref=src, dst_ref=dst, send_sem=send, recv_sem=recv_sem,
            device_id=(H * z + (q ^ e), c), device_id_type=MESH,
        )

    def geo_copy(e, which):
        src, dst = ((coords, coords_in), (quad, quad_in))[which]
        return to_core(
            e, src, dst.at[e - 1], geo_send.at[e - 1, which], geo_recv.at[e - 1, which]
        )

    def chunk_of(i):
        return pl.ds(*cuts[i])

    def slab_copy(e, i):
        lanes = chunk_of(i)
        return to_core(
            e, basis.at[pl.ds(0, local), lanes], basis.at[pl.ds(e * local, local), lanes],
            slab_send.at[e - 1, i], slab_recv.at[e - 1, i],
        )

    def node_copy(e):
        return to_core(
            e, nodes_out.at[e - 1], nodes_in.at[e - 1], node_send.at[e - 1], node_recv.at[e - 1]
        )

    for e in range(1, H):
        for which in range(2):
            geo_copy(e, which).start()
    for i in range(chunks):
        for e in range(1, H):
            slab_copy(e, i).start()
    for e in range(1, H):
        for which in range(2):
            geo_copy(e, which).wait_recv()
        fill_weights(e, coords_in.at[e - 1], quad_in.at[e - 1])

    part_id = lax.broadcasted_iota(jnp.int32, (rows, local), 0) // wl

    def scale(total, a, slot):
        lanes = pl.ds(slot * local, local)
        v = total * weights[a, :, lanes]
        turned = jnp.where(part_id == 0, pltpu.roll(v, rows - wl, 0), -pltpu.roll(v, wl, 0))
        scaled[:, lanes] = turned.astype(jnp.bfloat16)

    total = jnp.zeros((H * rows, local), jnp.float32)
    for d in range(C):
        s = c ^ d
        lanes = pl.ds(pl.multiple_of(s * width, width), width)
        for e in range(H):
            pltpu.make_async_copy(start, landed.at[e, s], first_recv.at[e, s]).wait()
            for x in range(2):
                field[pl.ds(e * rows + x * wl, wl), lanes] = landed[e, s, x].astype(jnp.float32)
        block = field[:, lanes].astype(jnp.bfloat16)
        cur[:, lanes] = block[:rows, :]
        total = total + lax.dot_general(
            block, basis[pl.ds(0, local), lanes], NT, preferred_element_type=jnp.float32
        )
    for e in range(1, H):
        nodes_out[e - 1] = total[e * rows : (e + 1) * rows, :]
        node_copy(e).start()
    scale(total[:rows, :], 0, 0)

    def part_copy(p, d, i):
        return pltpu.make_async_remote_copy(
            src_ref=parts.at[p, :, chunk_of(i)], dst_ref=recv.at[p, d - 1, :, chunk_of(i)],
            send_sem=part_send.at[p, d - 1, i], recv_sem=part_recv.at[p, d - 1, i],
            device_id=(H * (z ^ d) + q, c), device_id_type=MESH,
        )

    def send_part(p, i, block):
        parts[p, :, chunk_of(i)] = block.astype(jnp.bfloat16)
        for d in [1] + list(reversed(range(2, G))):
            part_copy(p, d, i).start()

    for i in range(chunks):
        early[:, chunk_of(i)] = lax.dot_general(
            scaled[:, pl.ds(0, local)], basis[pl.ds(0, local), chunk_of(i)], NN,
            preferred_element_type=jnp.float32,
        )
    for e in range(1, H):
        node_copy(e).wait_recv()
        scale(nodes_in[e - 1], 0, e)
    @pl.when(q != 0)
    def _():
        pl.semaphore_wait(turn, 1)

    for i in range(chunks):
        for e in range(1, H):
            slab_copy(e, i).wait_recv()
        send_part(0, i, early[:, chunk_of(i)] + lax.dot_general(
            scaled[:, pl.ds(local, (H - 1) * local)],
            basis[pl.ds(local, (H - 1) * local), chunk_of(i)], NN,
            preferred_element_type=jnp.float32,
        ))
    for d in range(1, G):
        part_copy(0, d, chunks - 1).wait_send()

    @pl.when(q != H - 1)
    def _():
        pl.semaphore_signal(
            turn, inc=1, device_id=(H * z + lax.rem(q + 1, H), c), device_id_type=MESH
        )

    def finish(step):
        p = lax.rem(step, 2)
        odd = p == 1
        factor = jnp.where(odd, 1.0, 0.5).astype(jnp.float32)
        for i in range(chunks):
            lanes = chunk_of(i)
            ready[:, lanes] = (
                field[pl.ds(0, rows), lanes]
                - (factor * lam[:, lanes]) * cur[:, lanes].astype(jnp.float32)
                + parts[p, :, lanes].astype(jnp.float32)
            )
        total = jnp.zeros((rows, H * local), jnp.float32)
        for i in range(chunks):
            lanes = chunk_of(i)
            acc = ready[:, lanes]
            for d in range(1, G):
                part_copy(p, d, i).wait_recv()
                acc = acc + recv[p, d - 1, :, lanes].astype(jnp.float32)
            rounded = acc.astype(jnp.bfloat16)
            cur[:, lanes] = rounded
            field[pl.ds(0, rows), lanes] = jnp.where(
                odd, rounded.astype(jnp.float32), field[pl.ds(0, rows), lanes]
            )
            total = total + lax.dot_general(
                rounded, basis[:, lanes], NT, preferred_element_type=jnp.float32
            )
        for slot in range(H):
            scale(total[:, slot * local : (slot + 1) * local], step + 1, slot)

    def sent(p, count):
        for i in range(count):
            for d in range(1, G):
                part_copy(p, d, i).wait_send()

    def half_step(step, carry):
        finish(step)
        p = lax.rem(step, 2)
        v = scaled[...]
        for i in range(chunks):
            send_part(1 - p, i, lax.dot_general(
                v, basis[:, chunk_of(i)], NN, preferred_element_type=jnp.float32
            ))
        sent(p, chunks - 1)

        @pl.when(step > 0)
        def _():
            for d in range(1, G):
                part_copy(p, d, chunks - 1).wait_send()

        return carry

    lax.fori_loop(0, halves - 2, half_step, 0)
    finish(halves - 2)

    def last_copy(d):
        return pltpu.make_async_remote_copy(
            src_ref=lastout.at[d], dst_ref=lastin.at[z], send_sem=last_send.at[d],
            recv_sem=last_recv.at[z], device_id=(H * c + q, c ^ d), device_id_type=MESH,
        )

    v = scaled[...]
    for d in reversed(range(C)):
        lanes = pl.ds(pl.multiple_of((c ^ d) * width, width), width)
        rest = field[pl.ds(0, rows), lanes] - lam[:, lanes] * cur[:, lanes].astype(jnp.float32)
        block = lax.dot_general(v, basis[:, lanes], NN, preferred_element_type=jnp.float32)
        lastout[d] = (block + jnp.where(is_self, rest, 0.0)).astype(jnp.bfloat16)
        if d:
            last_copy(d).start()
    unless(is_self, lambda: last_copy(0).start())

    @pl.when(is_self)
    def _():
        pltpu.make_async_copy(lastout.at[0], lastin.at[z], last_recv.at[z]).start()

    fresh = jnp.zeros((rows, width), jnp.float32)
    for s in range(G):
        pltpu.make_async_copy(lastout.at[0], lastin.at[s], last_recv.at[s]).wait()
        fresh = fresh + lastin[s].astype(jnp.float32)
    for x in range(2):
        out[x] = fresh[x * wl : (x + 1) * wl, :].astype(jnp.bfloat16)

    sent((halves - 2) % 2, chunks)
    for d in range(C):
        unless(is_self & (d == 0), lambda d=d: last_copy(d).wait_send())
    for d in range(G):
        for e in range(H):
            unless(is_self & (d + e == 0), lambda d=d, e=e: first_copy(d, e).wait_send())
    for e in range(1, H):
        node_copy(e).wait_send()
        for which in range(2):
            geo_copy(e, which).wait_send()
        for i in range(chunks):
            slab_copy(e, i).wait_send()


def on_device(R, C, basis, coords, quad, magnetization, rates, dirs):
    H = R // C
    G = R // H
    local, M = basis.shape
    start = jnp.transpose(magnetization, (0, 2, 1))
    quad = quad.reshape(-1, 128)
    rates = rates.reshape(-1, 128)
    _, wl, width = start.shape
    rows = 2 * wl
    cuts = cuts_of(M)
    chunks = len(cuts)
    dma = pltpu.SemaphoreType.DMA
    bf16, f32 = jnp.bfloat16, jnp.float32
    result = pl.pallas_call(
        functools.partial(kernel, R, C),
        out_shape=pltpu.VMEM(start.shape, bf16),
        in_specs=[pl.BlockSpec(memory_space=pl.ANY)] * 6,
        out_specs=pl.BlockSpec(memory_space=pltpu.VMEM),
        scratch_shapes=[
            pltpu.VMEM((H * local, M), bf16),
            pltpu.VMEM(coords.shape, f32),
            pltpu.VMEM(quad.shape, f32),
            pltpu.VMEM(rates.shape, f32),
            pltpu.VMEM(dirs.shape, f32),
            pltpu.VMEM((H, C, 2, wl, width), bf16),
            pltpu.VMEM((rows, M), bf16),
            pltpu.VMEM((H * rows, M), f32),
            pltpu.VMEM((rows, M), f32),
            pltpu.VMEM((rows, M), f32),
            pltpu.VMEM((rows, M), f32),
            pltpu.VMEM((2, rows, M), bf16),
            pltpu.VMEM((2, G - 1, rows, M), bf16),
            pltpu.VMEM((2 * STEPS, rows, H * local), f32),
            pltpu.VMEM((H - 1,) + coords.shape, f32),
            pltpu.VMEM((H - 1,) + quad.shape, f32),
            pltpu.VMEM((H - 1, rows, local), f32),
            pltpu.VMEM((H - 1, rows, local), f32),
            pltpu.VMEM((rows, H * local), bf16),
            pltpu.VMEM((C, rows, width), bf16),
            pltpu.VMEM((G, rows, width), bf16),
            dma((5,)),
            dma((H - 1, chunks)), dma((H - 1, chunks)),
            dma((H - 1, 2)), dma((H - 1, 2)),
            dma((G, H)), dma((H, C)),
            dma((H - 1,)), dma((H - 1,)),
            pltpu.SemaphoreType.REGULAR,
            dma((2, G - 1, chunks)), dma((2, G - 1, chunks)),
            dma((C,)), dma((G,)),
        ],
        compiler_params=pltpu.CompilerParams(collective_id=0, has_side_effects=True),
    )(basis, coords, quad, start, rates, dirs)
    return jnp.transpose(result, (0, 2, 1))


def solution(mesh):
    return jax.shard_map(
        functools.partial(on_device, mesh.shape["row"], mesh.shape["col"]),
        mesh=mesh,
        in_specs=(P("row", None), P(None, "row"), P("row"), P(None, "col", "row"), P(), P()),
        out_specs=P(None, "col", "row"),
        check_vma=False,
    )
```

```python
import functools

import jax
import jax.numpy as jnp
from jax import lax
from jax.experimental import pallas as pl
from jax.experimental.pallas import tpu as pltpu
from jax.sharding import PartitionSpec as P

STEPS = 3
CHUNKS = (512,) * 8
MESH = pl.DeviceIdType.MESH
NT = (((1,), (1,)), ((), ()))
NN = (((1,), (0,)), ((), ()))


def cuts_of(M):
    starts = [sum(CHUNKS[:i]) for i in range(len(CHUNKS))]
    return list(zip(starts, CHUNKS))


def kernel(
    R, C, basis_hbm, coords_hbm, quad_hbm, start, rates_hbm, dirs_hbm, out,
    basis, coords, quad, rates, dirs, landed, cur, field, ready, lam, early, parts, recv, weights,
    coords_in, quad_in, nodes_out, nodes_in, scaled, lastout, lastin,
    load_sem, slab_send, slab_recv, geo_send, geo_recv, first_send, first_recv,
    node_send, node_recv, turn, part_send, part_recv, last_send, last_recv,
):
    H = R // C
    G = R // H
    r = lax.axis_index("row")
    c = lax.axis_index("col")
    z = r // H
    q = lax.rem(r, H)
    wl, width = start.shape[1], start.shape[2]
    rows = 2 * wl
    local = basis_hbm.shape[0]
    M = basis_hbm.shape[1]
    halves = 2 * STEPS
    cuts = cuts_of(M)
    chunks = len(cuts)

    barrier = pltpu.get_barrier_semaphore()
    is_self = z == c

    def greet(row, col):
        pl.semaphore_signal(barrier, inc=1, device_id=(row, col), device_id_type=MESH)

    def unless(cond, fn):
        pl.when(jnp.logical_not(cond))(fn)

    for d in reversed(range(C)):
        for e in range(H):
            unless(is_self & (d + e == 0), functools.partial(greet, H * c + (q ^ e), c ^ d))
    for d in reversed(range(G)):
        for e in range(H):
            unless(is_self & (d + e == 0), functools.partial(greet, H * (z ^ d) + (q ^ e), z))
    for d in range(1, G):
        greet(H * (z ^ d) + q, c)
    for e in range(1, H):
        greet(H * z + (q ^ e), c)

    loads = [
        pltpu.make_async_copy(src, dst, load_sem.at[k])
        for k, (src, dst) in enumerate((
            (coords_hbm, coords), (quad_hbm, quad), (rates_hbm, rates), (dirs_hbm, dirs),
            (basis_hbm, basis.at[pl.ds(0, local), :]),
        ))
    ]
    for load in loads:
        load.start()
    for load in loads[:-1]:
        load.wait()

    row_id = lax.broadcasted_iota(jnp.int32, (rows, dirs.shape[2]), 0)
    wave_id = lax.broadcasted_iota(jnp.int32, (rows, dirs.shape[2]), 1)
    chosen = wave_id == (H * c + q) * wl + row_id % wl

    def fill_weights(slot, xyz, qw):
        for a in range(halves):
            column = [
                (1.0 if a % 2 else 0.5)
                * jnp.sum(jnp.where(chosen, dirs[a, k : k + 1, :], 0.0), axis=1, keepdims=True)
                for k in range(3)
            ]
            for i in range(local // 128):
                lanes = pl.ds(i * 128, 128)
                w = qw[i : i + 1, :]
                weights[a, :, pl.ds(slot * local + i * 128, 128)] = (
                    column[0] * (xyz[0:1, lanes] * w)
                    + column[1] * (xyz[1:2, lanes] * w)
                    + column[2] * (xyz[2:3, lanes] * w)
                )

    fill_weights(0, coords, quad)
    for i in range(M // 128):
        lam[:, pl.ds(i * 128, 128)] = jnp.broadcast_to(rates[i : i + 1, :], (rows, 128))
    loads[-1].wait()

    pl.semaphore_wait(barrier, H * C + R + G - 1 + H - 1 - 2 * is_self.astype(jnp.int32))

    def first_copy(d, e):
        return pltpu.make_async_remote_copy(
            src_ref=start, dst_ref=landed.at[e, c], send_sem=first_send.at[d, e],
            recv_sem=first_recv.at[e, c], device_id=(H * (z ^ d) + (q ^ e), z),
            device_id_type=MESH,
        )

    for d in reversed(range(G)):
        for e in reversed(range(H)):
            unless(is_self & (d + e == 0), lambda d=d, e=e: first_copy(d, e).start())

    @pl.when(is_self)
    def _():
        pltpu.make_async_copy(start, landed.at[0, c], first_recv.at[0, c]).start()

    def to_core(e, src, dst, send, recv_sem):
        return pltpu.make_async_remote_copy(
            src_ref=src, dst_ref=dst, send_sem=send, recv_sem=recv_sem,
            device_id=(H * z + (q ^ e), c), device_id_type=MESH,
        )

    def geo_copy(e, which):
        src, dst = ((coords, coords_in), (quad, quad_in))[which]
        return to_core(
            e, src, dst.at[e - 1], geo_send.at[e - 1, which], geo_recv.at[e - 1, which]
        )

    def chunk_of(i):
        return pl.ds(*cuts[i])

    def slab_copy(e, i):
        lanes = chunk_of(i)
        return to_core(
            e, basis.at[pl.ds(0, local), lanes], basis.at[pl.ds(e * local, local), lanes],
            slab_send.at[e - 1, i], slab_recv.at[e - 1, i],
        )

    def node_copy(e):
        return to_core(
            e, nodes_out.at[e - 1], nodes_in.at[e - 1], node_send.at[e - 1], node_recv.at[e - 1]
        )

    for e in range(1, H):
        for which in range(2):
            geo_copy(e, which).start()
    for i in range(chunks):
        for e in range(1, H):
            slab_copy(e, i).start()
    for e in range(1, H):
        for which in range(2):
            geo_copy(e, which).wait_recv()
        fill_weights(e, coords_in.at[e - 1], quad_in.at[e - 1])

    part_id = lax.broadcasted_iota(jnp.int32, (rows, local), 0) // wl

    def scale(total, a, slot):
        lanes = pl.ds(slot * local, local)
        v = total * weights[a, :, lanes]
        turned = jnp.where(part_id == 0, pltpu.roll(v, rows - wl, 0), -pltpu.roll(v, wl, 0))
        scaled[:, lanes] = turned.astype(jnp.bfloat16)

    total = jnp.zeros((H * rows, local), jnp.float32)
    for d in range(C):
        s = c ^ d
        lanes = pl.ds(pl.multiple_of(s * width, width), width)
        for e in range(H):
            pltpu.make_async_copy(start, landed.at[e, s], first_recv.at[e, s]).wait()
            for x in range(2):
                field[pl.ds(e * rows + x * wl, wl), lanes] = landed[e, s, x].astype(jnp.float32)
        block = field[:, lanes].astype(jnp.bfloat16)
        cur[:, lanes] = block[:rows, :]
        total = total + lax.dot_general(
            block, basis[pl.ds(0, local), lanes], NT, preferred_element_type=jnp.float32
        )
    for e in range(1, H):
        nodes_out[e - 1] = total[e * rows : (e + 1) * rows, :]
        node_copy(e).start()
    scale(total[:rows, :], 0, 0)

    def part_copy(p, d, i):
        return pltpu.make_async_remote_copy(
            src_ref=parts.at[p, :, chunk_of(i)], dst_ref=recv.at[p, d - 1, :, chunk_of(i)],
            send_sem=part_send.at[p, d - 1, i], recv_sem=part_recv.at[p, d - 1, i],
            device_id=(H * (z ^ d) + q, c), device_id_type=MESH,
        )

    def send_part(p, i, block):
        parts[p, :, chunk_of(i)] = block.astype(jnp.bfloat16)
        for d in [1] + list(reversed(range(2, G))):
            part_copy(p, d, i).start()

    for i in range(chunks):
        early[:, chunk_of(i)] = lax.dot_general(
            scaled[:, pl.ds(0, local)], basis[pl.ds(0, local), chunk_of(i)], NN,
            preferred_element_type=jnp.float32,
        )
    for e in range(1, H):
        node_copy(e).wait_recv()
        scale(nodes_in[e - 1], 0, e)
    @pl.when(q != 0)
    def _():
        pl.semaphore_wait(turn, 1)

    for i in range(chunks):
        for e in range(1, H):
            slab_copy(e, i).wait_recv()
        send_part(0, i, early[:, chunk_of(i)] + lax.dot_general(
            scaled[:, pl.ds(local, (H - 1) * local)],
            basis[pl.ds(local, (H - 1) * local), chunk_of(i)], NN,
            preferred_element_type=jnp.float32,
        ))
    @pl.when(q != H - 1)
    def _():
        for d in range(1, G):
            part_copy(0, d, chunks - 1).wait_send()
        pl.semaphore_signal(
            turn, inc=1, device_id=(H * z + lax.rem(q + 1, H), c), device_id_type=MESH
        )

    def finish(step):
        p = lax.rem(step, 2)
        odd = p == 1
        factor = jnp.where(odd, 1.0, 0.5).astype(jnp.float32)
        for i in range(chunks):
            lanes = chunk_of(i)
            ready[:, lanes] = (
                field[pl.ds(0, rows), lanes]
                - (factor * lam[:, lanes]) * cur[:, lanes].astype(jnp.float32)
                + parts[p, :, lanes].astype(jnp.float32)
            )
        total = jnp.zeros((rows, H * local), jnp.float32)
        for i in range(chunks):
            lanes = chunk_of(i)
            acc = ready[:, lanes]
            for d in range(1, G):
                part_copy(p, d, i).wait_recv()
                acc = acc + recv[p, d - 1, :, lanes].astype(jnp.float32)
            rounded = acc.astype(jnp.bfloat16)
            cur[:, lanes] = rounded
            field[pl.ds(0, rows), lanes] = jnp.where(
                odd, rounded.astype(jnp.float32), field[pl.ds(0, rows), lanes]
            )
            total = total + lax.dot_general(
                rounded, basis[:, lanes], NT, preferred_element_type=jnp.float32
            )
        for slot in range(H):
            scale(total[:, slot * local : (slot + 1) * local], step + 1, slot)

    def sent(p, count):
        for i in range(count):
            for d in range(1, G):
                part_copy(p, d, i).wait_send()

    def half_step(step, carry):
        finish(step)
        p = lax.rem(step, 2)
        v = scaled[...]
        for i in range(chunks):
            send_part(1 - p, i, lax.dot_general(
                v, basis[:, chunk_of(i)], NN, preferred_element_type=jnp.float32
            ))
        sent(p, chunks - 1)

        @pl.when((step > 0) | (q == H - 1))
        def _():
            for d in range(1, G):
                part_copy(p, d, chunks - 1).wait_send()

        return carry

    lax.fori_loop(0, halves - 2, half_step, 0)
    finish(halves - 2)

    def last_copy(d):
        return pltpu.make_async_remote_copy(
            src_ref=lastout.at[d], dst_ref=lastin.at[z], send_sem=last_send.at[d],
            recv_sem=last_recv.at[z], device_id=(H * c + q, c ^ d), device_id_type=MESH,
        )

    v = scaled[...]
    for d in reversed(range(C)):
        lanes = pl.ds(pl.multiple_of((c ^ d) * width, width), width)
        rest = field[pl.ds(0, rows), lanes] - lam[:, lanes] * cur[:, lanes].astype(jnp.float32)
        block = lax.dot_general(v, basis[:, lanes], NN, preferred_element_type=jnp.float32)
        lastout[d] = (block + jnp.where(is_self, rest, 0.0)).astype(jnp.bfloat16)
        if d:
            last_copy(d).start()
    unless(is_self, lambda: last_copy(0).start())

    @pl.when(is_self)
    def _():
        pltpu.make_async_copy(lastout.at[0], lastin.at[z], last_recv.at[z]).start()

    fresh = jnp.zeros((rows, width), jnp.float32)
    for s in range(G):
        pltpu.make_async_copy(lastout.at[0], lastin.at[s], last_recv.at[s]).wait()
        fresh = fresh + lastin[s].astype(jnp.float32)
    for x in range(2):
        out[x] = fresh[x * wl : (x + 1) * wl, :].astype(jnp.bfloat16)

    sent((halves - 2) % 2, chunks)
    for d in range(C):
        unless(is_self & (d == 0), lambda d=d: last_copy(d).wait_send())
    for d in range(G):
        for e in range(H):
            unless(is_self & (d + e == 0), lambda d=d, e=e: first_copy(d, e).wait_send())
    for e in range(1, H):
        node_copy(e).wait_send()
        for which in range(2):
            geo_copy(e, which).wait_send()
        for i in range(chunks):
            slab_copy(e, i).wait_send()


def on_device(R, C, basis, coords, quad, magnetization, rates, dirs):
    H = R // C
    G = R // H
    local, M = basis.shape
    start = jnp.transpose(magnetization, (0, 2, 1))
    quad = quad.reshape(-1, 128)
    rates = rates.reshape(-1, 128)
    _, wl, width = start.shape
    rows = 2 * wl
    cuts = cuts_of(M)
    chunks = len(cuts)
    dma = pltpu.SemaphoreType.DMA
    bf16, f32 = jnp.bfloat16, jnp.float32
    result = pl.pallas_call(
        functools.partial(kernel, R, C),
        out_shape=pltpu.VMEM(start.shape, bf16),
        in_specs=[pl.BlockSpec(memory_space=pl.ANY)] * 6,
        out_specs=pl.BlockSpec(memory_space=pltpu.VMEM),
        scratch_shapes=[
            pltpu.VMEM((H * local, M), bf16),
            pltpu.VMEM(coords.shape, f32),
            pltpu.VMEM(quad.shape, f32),
            pltpu.VMEM(rates.shape, f32),
            pltpu.VMEM(dirs.shape, f32),
            pltpu.VMEM((H, C, 2, wl, width), bf16),
            pltpu.VMEM((rows, M), bf16),
            pltpu.VMEM((H * rows, M), f32),
            pltpu.VMEM((rows, M), f32),
            pltpu.VMEM((rows, M), f32),
            pltpu.VMEM((rows, M), f32),
            pltpu.VMEM((2, rows, M), bf16),
            pltpu.VMEM((2, G - 1, rows, M), bf16),
            pltpu.VMEM((2 * STEPS, rows, H * local), f32),
            pltpu.VMEM((H - 1,) + coords.shape, f32),
            pltpu.VMEM((H - 1,) + quad.shape, f32),
            pltpu.VMEM((H - 1, rows, local), f32),
            pltpu.VMEM((H - 1, rows, local), f32),
            pltpu.VMEM((rows, H * local), bf16),
            pltpu.VMEM((C, rows, width), bf16),
            pltpu.VMEM((G, rows, width), bf16),
            dma((5,)),
            dma((H - 1, chunks)), dma((H - 1, chunks)),
            dma((H - 1, 2)), dma((H - 1, 2)),
            dma((G, H)), dma((H, C)),
            dma((H - 1,)), dma((H - 1,)),
            pltpu.SemaphoreType.REGULAR,
            dma((2, G - 1, chunks)), dma((2, G - 1, chunks)),
            dma((C,)), dma((G,)),
        ],
        compiler_params=pltpu.CompilerParams(collective_id=0, has_side_effects=True),
    )(basis, coords, quad, start, rates, dirs)
    return jnp.transpose(result, (0, 2, 1))


def solution(mesh):
    return jax.shard_map(
        functools.partial(on_device, mesh.shape["row"], mesh.shape["col"]),
        mesh=mesh,
        in_specs=(P("row", None), P(None, "row"), P("row"), P(None, "col", "row"), P(), P()),
        out_specs=P(None, "col", "row"),
        check_vma=False,
    )
```

```python
import functools

import jax
import jax.numpy as jnp
from jax import lax
from jax.experimental import pallas as pl
from jax.experimental.pallas import tpu as pltpu
from jax.sharding import PartitionSpec as P

STEPS = 3
CHUNK = 512
MESH = pl.DeviceIdType.MESH
NT = (((1,), (1,)), ((), ()))
NN = (((1,), (0,)), ((), ()))


def cuts_of(M):
    return [(i * CHUNK, CHUNK) for i in range(M // CHUNK)]


def kernel(
    R, C, basis_hbm, coords_hbm, quad_hbm, start, rates_hbm, dirs_hbm, out,
    basis, coords, quad, rates, dirs, landed, cur, field, ready, lam, early, parts, recv, weights,
    coords_in, quad_in, nodes_out, nodes_in, scaled, lastout, lastin,
    load_sem, slab_send, slab_recv, geo_send, geo_recv, first_send, first_recv,
    node_send, node_recv, turn, part_send, part_recv, last_send, last_recv,
):
    H = R // C
    G = R // H
    r = lax.axis_index("row")
    c = lax.axis_index("col")
    z = r // H
    q = lax.rem(r, H)
    wl, width = start.shape[1], start.shape[2]
    rows = 2 * wl
    local = basis_hbm.shape[0]
    M = basis_hbm.shape[1]
    halves = 2 * STEPS
    cuts = cuts_of(M)
    chunks = len(cuts)

    barrier = pltpu.get_barrier_semaphore()
    is_self = z == c

    def greet(row, col):
        pl.semaphore_signal(barrier, inc=1, device_id=(row, col), device_id_type=MESH)

    def unless(cond, fn):
        pl.when(jnp.logical_not(cond))(fn)

    for d in reversed(range(C)):
        for e in range(H):
            unless(is_self & (d + e == 0), functools.partial(greet, H * c + (q ^ e), c ^ d))
    for d in reversed(range(G)):
        for e in range(H):
            unless(is_self & (d + e == 0), functools.partial(greet, H * (z ^ d) + (q ^ e), z))
    for d in range(1, G):
        greet(H * (z ^ d) + q, c)
    for e in range(1, H):
        greet(H * z + (q ^ e), c)

    loads = [
        pltpu.make_async_copy(src, dst, load_sem.at[k])
        for k, (src, dst) in enumerate((
            (coords_hbm, coords), (quad_hbm, quad), (rates_hbm, rates), (dirs_hbm, dirs),
            (basis_hbm, basis.at[pl.ds(0, local), :]),
        ))
    ]
    for load in loads:
        load.start()
    for load in loads[:-1]:
        load.wait()

    row_id = lax.broadcasted_iota(jnp.int32, (rows, dirs.shape[2]), 0)
    wave_id = lax.broadcasted_iota(jnp.int32, (rows, dirs.shape[2]), 1)
    chosen = wave_id == (H * c + q) * wl + row_id % wl

    def fill_weights(slot, xyz, qw):
        for a in range(halves):
            column = [
                (1.0 if a % 2 else 0.5)
                * jnp.sum(jnp.where(chosen, dirs[a, k : k + 1, :], 0.0), axis=1, keepdims=True)
                for k in range(3)
            ]
            for i in range(local // 128):
                lanes = pl.ds(i * 128, 128)
                w = qw[i : i + 1, :]
                weights[a, :, pl.ds(slot * local + i * 128, 128)] = (
                    column[0] * (xyz[0:1, lanes] * w)
                    + column[1] * (xyz[1:2, lanes] * w)
                    + column[2] * (xyz[2:3, lanes] * w)
                )

    fill_weights(0, coords, quad)
    for i in range(M // 128):
        lam[:, pl.ds(i * 128, 128)] = jnp.broadcast_to(rates[i : i + 1, :], (rows, 128))
    loads[-1].wait()

    pl.semaphore_wait(barrier, H * C + R + G - 1 + H - 1 - 2 * is_self.astype(jnp.int32))

    def first_copy(d, e):
        return pltpu.make_async_remote_copy(
            src_ref=start, dst_ref=landed.at[e, c], send_sem=first_send.at[d, e],
            recv_sem=first_recv.at[e, c], device_id=(H * (z ^ d) + (q ^ e), z),
            device_id_type=MESH,
        )

    for d in reversed(range(G)):
        for e in reversed(range(H)):
            unless(is_self & (d + e == 0), lambda d=d, e=e: first_copy(d, e).start())

    @pl.when(is_self)
    def _():
        pltpu.make_async_copy(start, landed.at[0, c], first_recv.at[0, c]).start()

    def to_core(e, src, dst, send, recv_sem):
        return pltpu.make_async_remote_copy(
            src_ref=src, dst_ref=dst, send_sem=send, recv_sem=recv_sem,
            device_id=(H * z + (q ^ e), c), device_id_type=MESH,
        )

    def geo_copy(e, which):
        src, dst = ((coords, coords_in), (quad, quad_in))[which]
        return to_core(
            e, src, dst.at[e - 1], geo_send.at[e - 1, which], geo_recv.at[e - 1, which]
        )

    def chunk_of(i):
        return pl.ds(*cuts[i])

    def slab_copy(e, i):
        lanes = chunk_of(i)
        return to_core(
            e, basis.at[pl.ds(0, local), lanes], basis.at[pl.ds(e * local, local), lanes],
            slab_send.at[e - 1, i], slab_recv.at[e - 1, i],
        )

    def node_copy(e):
        return to_core(
            e, nodes_out.at[e - 1], nodes_in.at[e - 1], node_send.at[e - 1], node_recv.at[e - 1]
        )

    for e in range(1, H):
        for which in range(2):
            geo_copy(e, which).start()
    for i in range(chunks):
        for e in range(1, H):
            slab_copy(e, i).start()
    for e in range(1, H):
        for which in range(2):
            geo_copy(e, which).wait_recv()
        fill_weights(e, coords_in.at[e - 1], quad_in.at[e - 1])

    part_id = lax.broadcasted_iota(jnp.int32, (rows, local), 0) // wl

    def scale(total, a, slot):
        lanes = pl.ds(slot * local, local)
        v = total * weights[a, :, lanes]
        turned = jnp.where(part_id == 0, pltpu.roll(v, rows - wl, 0), -pltpu.roll(v, wl, 0))
        scaled[:, lanes] = turned.astype(jnp.bfloat16)

    total = jnp.zeros((H * rows, local), jnp.float32)
    for d in range(C):
        s = c ^ d
        lanes = pl.ds(pl.multiple_of(s * width, width), width)
        for e in range(H):
            pltpu.make_async_copy(start, landed.at[e, s], first_recv.at[e, s]).wait()
            for x in range(2):
                field[pl.ds(e * rows + x * wl, wl), lanes] = landed[e, s, x].astype(jnp.float32)
        block = field[:, lanes].astype(jnp.bfloat16)
        cur[:, lanes] = block[:rows, :]
        total = total + lax.dot_general(
            block, basis[pl.ds(0, local), lanes], NT, preferred_element_type=jnp.float32
        )
    for e in range(1, H):
        nodes_out[e - 1] = total[e * rows : (e + 1) * rows, :]
        node_copy(e).start()
    scale(total[:rows, :], 0, 0)

    def part_copy(p, d, i):
        return pltpu.make_async_remote_copy(
            src_ref=parts.at[p, :, chunk_of(i)], dst_ref=recv.at[p, d - 1, :, chunk_of(i)],
            send_sem=part_send.at[p, d - 1, i], recv_sem=part_recv.at[p, d - 1, i],
            device_id=(H * (z ^ d) + q, c), device_id_type=MESH,
        )

    def send_part(p, i, block):
        parts[p, :, chunk_of(i)] = block.astype(jnp.bfloat16)
        for d in [1] + list(reversed(range(2, G))):
            part_copy(p, d, i).start()

    for i in range(chunks):
        early[:, chunk_of(i)] = lax.dot_general(
            scaled[:, pl.ds(0, local)], basis[pl.ds(0, local), chunk_of(i)], NN,
            preferred_element_type=jnp.float32,
        )
    for e in range(1, H):
        node_copy(e).wait_recv()
        scale(nodes_in[e - 1], 0, e)
    @pl.when(q != 0)
    def _():
        pl.semaphore_wait(turn, 1)

    for i in range(chunks):
        for e in range(1, H):
            slab_copy(e, i).wait_recv()
        send_part(0, i, early[:, chunk_of(i)] + lax.dot_general(
            scaled[:, pl.ds(local, (H - 1) * local)],
            basis[pl.ds(local, (H - 1) * local), chunk_of(i)], NN,
            preferred_element_type=jnp.float32,
        ))
    @pl.when(q != H - 1)
    def _():
        for d in range(1, G):
            part_copy(0, d, chunks - 1).wait_send()
        pl.semaphore_signal(
            turn, inc=1, device_id=(H * z + lax.rem(q + 1, H), c), device_id_type=MESH
        )

    def finish(step):
        p = lax.rem(step, 2)
        odd = p == 1
        factor = jnp.where(odd, 1.0, 0.5).astype(jnp.float32)
        for i in range(chunks):
            lanes = chunk_of(i)
            ready[:, lanes] = (
                field[pl.ds(0, rows), lanes]
                - (factor * lam[:, lanes]) * cur[:, lanes].astype(jnp.float32)
                + parts[p, :, lanes].astype(jnp.float32)
            )
        total = jnp.zeros((rows, H * local), jnp.float32)
        for i in range(chunks):
            lanes = chunk_of(i)
            acc = ready[:, lanes]
            for d in range(1, G):
                part_copy(p, d, i).wait_recv()
                acc = acc + recv[p, d - 1, :, lanes].astype(jnp.float32)
            rounded = acc.astype(jnp.bfloat16)
            cur[:, lanes] = rounded
            field[pl.ds(0, rows), lanes] = jnp.where(
                odd, rounded.astype(jnp.float32), field[pl.ds(0, rows), lanes]
            )
            total = total + lax.dot_general(
                rounded, basis[:, lanes], NT, preferred_element_type=jnp.float32
            )
        for slot in range(H):
            scale(total[:, slot * local : (slot + 1) * local], step + 1, slot)

    def sent(p, count):
        for i in range(count):
            for d in range(1, G):
                part_copy(p, d, i).wait_send()

    def half_step(step, carry):
        finish(step)
        p = lax.rem(step, 2)
        v = scaled[...]
        for i in range(chunks):
            send_part(1 - p, i, lax.dot_general(
                v, basis[:, chunk_of(i)], NN, preferred_element_type=jnp.float32
            ))
        sent(p, chunks - 1)

        @pl.when((step > 0) | (q == H - 1))
        def _():
            for d in range(1, G):
                part_copy(p, d, chunks - 1).wait_send()

        return carry

    lax.fori_loop(0, halves - 2, half_step, 0)
    finish(halves - 2)

    def last_copy(d):
        return pltpu.make_async_remote_copy(
            src_ref=lastout.at[d], dst_ref=lastin.at[z], send_sem=last_send.at[d],
            recv_sem=last_recv.at[z], device_id=(H * c + q, c ^ d), device_id_type=MESH,
        )

    v = scaled[...]
    for d in reversed(range(C)):
        lanes = pl.ds(pl.multiple_of((c ^ d) * width, width), width)
        rest = field[pl.ds(0, rows), lanes] - lam[:, lanes] * cur[:, lanes].astype(jnp.float32)
        block = lax.dot_general(v, basis[:, lanes], NN, preferred_element_type=jnp.float32)
        lastout[d] = (block + jnp.where(is_self, rest, 0.0)).astype(jnp.bfloat16)
        if d:
            last_copy(d).start()
    unless(is_self, lambda: last_copy(0).start())

    @pl.when(is_self)
    def _():
        pltpu.make_async_copy(lastout.at[0], lastin.at[z], last_recv.at[z]).start()

    fresh = jnp.zeros((rows, width), jnp.float32)
    for s in range(G):
        pltpu.make_async_copy(lastout.at[0], lastin.at[s], last_recv.at[s]).wait()
        fresh = fresh + lastin[s].astype(jnp.float32)
    for x in range(2):
        out[x] = fresh[x * wl : (x + 1) * wl, :].astype(jnp.bfloat16)

    sent((halves - 2) % 2, chunks)
    for d in range(C):
        unless(is_self & (d == 0), lambda d=d: last_copy(d).wait_send())
    for d in range(G):
        for e in range(H):
            unless(is_self & (d + e == 0), lambda d=d, e=e: first_copy(d, e).wait_send())
    for e in range(1, H):
        node_copy(e).wait_send()
        for which in range(2):
            geo_copy(e, which).wait_send()
        for i in range(chunks):
            slab_copy(e, i).wait_send()


def on_device(R, C, basis, coords, quad, magnetization, rates, dirs):
    H = R // C
    G = R // H
    local, M = basis.shape
    start = jnp.transpose(magnetization, (0, 2, 1))
    quad = quad.reshape(-1, 128)
    rates = rates.reshape(-1, 128)
    _, wl, width = start.shape
    rows = 2 * wl
    cuts = cuts_of(M)
    chunks = len(cuts)
    dma = pltpu.SemaphoreType.DMA
    bf16, f32 = jnp.bfloat16, jnp.float32
    result = pl.pallas_call(
        functools.partial(kernel, R, C),
        out_shape=pltpu.VMEM(start.shape, bf16),
        in_specs=[pl.BlockSpec(memory_space=pl.ANY)] * 6,
        out_specs=pl.BlockSpec(memory_space=pltpu.VMEM),
        scratch_shapes=[
            pltpu.VMEM((H * local, M), bf16),
            pltpu.VMEM(coords.shape, f32),
            pltpu.VMEM(quad.shape, f32),
            pltpu.VMEM(rates.shape, f32),
            pltpu.VMEM(dirs.shape, f32),
            pltpu.VMEM((H, C, 2, wl, width), bf16),
            pltpu.VMEM((rows, M), bf16),
            pltpu.VMEM((H * rows, M), f32),
            pltpu.VMEM((rows, M), f32),
            pltpu.VMEM((rows, M), f32),
            pltpu.VMEM((rows, M), f32),
            pltpu.VMEM((2, rows, M), bf16),
            pltpu.VMEM((2, G - 1, rows, M), bf16),
            pltpu.VMEM((2 * STEPS, rows, H * local), f32),
            pltpu.VMEM((H - 1,) + coords.shape, f32),
            pltpu.VMEM((H - 1,) + quad.shape, f32),
            pltpu.VMEM((H - 1, rows, local), f32),
            pltpu.VMEM((H - 1, rows, local), f32),
            pltpu.VMEM((rows, H * local), bf16),
            pltpu.VMEM((C, rows, width), bf16),
            pltpu.VMEM((G, rows, width), bf16),
            dma((5,)),
            dma((H - 1, chunks)), dma((H - 1, chunks)),
            dma((H - 1, 2)), dma((H - 1, 2)),
            dma((G, H)), dma((H, C)),
            dma((H - 1,)), dma((H - 1,)),
            pltpu.SemaphoreType.REGULAR,
            dma((2, G - 1, chunks)), dma((2, G - 1, chunks)),
            dma((C,)), dma((G,)),
        ],
        compiler_params=pltpu.CompilerParams(collective_id=0, has_side_effects=True),
    )(basis, coords, quad, start, rates, dirs)
    return jnp.transpose(result, (0, 2, 1))


def solution(mesh):
    return jax.shard_map(
        functools.partial(on_device, mesh.shape["row"], mesh.shape["col"]),
        mesh=mesh,
        in_specs=(P("row", None), P(None, "row"), P("row"), P(None, "col", "row"), P(), P()),
        out_specs=P(None, "col", "row"),
        check_vma=False,
    )
```

```python
import functools

import jax
import jax.numpy as jnp
from jax import lax
from jax.experimental import pallas as pl
from jax.experimental.pallas import tpu as pltpu
from jax.sharding import PartitionSpec as P

STEPS = 3
CHUNK = 512
MESH = pl.DeviceIdType.MESH
NT = (((1,), (1,)), ((), ()))
NN = (((1,), (0,)), ((), ()))


def cuts_of(M):
    return [(i * CHUNK, CHUNK) for i in range(M // CHUNK)]


def kernel(
    R, C, basis_hbm, coords_hbm, quad_hbm, start, rates_hbm, dirs_hbm, out,
    basis, coords, quad, rates, dirs, landed, cur, field, ready, lam, early, parts, recv, weights,
    coords_in, quad_in, nodes_out, nodes_in, scaled, lastout, lastin,
    load_sem, slab_send, slab_recv, geo_send, geo_recv, first_send, first_recv,
    node_send, node_recv, turn, part_send, part_recv, last_send, last_recv,
):
    H = R // C
    G = R // H
    r = lax.axis_index("row")
    c = lax.axis_index("col")
    z = r // H
    q = lax.rem(r, H)
    wl, width = start.shape[1], start.shape[2]
    rows = 2 * wl
    local = basis_hbm.shape[0]
    M = basis_hbm.shape[1]
    halves = 2 * STEPS
    cuts = cuts_of(M)
    chunks = len(cuts)

    barrier = pltpu.get_barrier_semaphore()
    is_self = z == c

    def greet(row, col):
        pl.semaphore_signal(barrier, inc=1, device_id=(row, col), device_id_type=MESH)

    def unless(cond, fn):
        pl.when(jnp.logical_not(cond))(fn)

    for d in reversed(range(C)):
        for e in range(H):
            unless(is_self & (d + e == 0), functools.partial(greet, H * c + (q ^ e), c ^ d))
    for d in reversed(range(G)):
        for e in range(H):
            unless(is_self & (d + e == 0), functools.partial(greet, H * (z ^ d) + (q ^ e), z))
    for d in range(1, G):
        greet(H * (z ^ d) + q, c)
    for e in range(1, H):
        greet(H * z + (q ^ e), c)

    loads = [
        pltpu.make_async_copy(src, dst, load_sem.at[k])
        for k, (src, dst) in enumerate((
            (coords_hbm, coords), (quad_hbm, quad), (rates_hbm, rates), (dirs_hbm, dirs),
            (basis_hbm, basis.at[pl.ds(0, local), :]),
        ))
    ]
    for load in loads:
        load.start()
    for load in loads[:-1]:
        load.wait()

    row_id = lax.broadcasted_iota(jnp.int32, (rows, dirs.shape[2]), 0)
    wave_id = lax.broadcasted_iota(jnp.int32, (rows, dirs.shape[2]), 1)
    chosen = wave_id == (H * c + q) * wl + row_id % wl

    def fill_weights(slot, xyz, qw):
        for a in range(halves):
            column = [
                (1.0 if a % 2 else 0.5)
                * jnp.sum(jnp.where(chosen, dirs[a, k : k + 1, :], 0.0), axis=1, keepdims=True)
                for k in range(3)
            ]
            for i in range(local // 128):
                lanes = pl.ds(i * 128, 128)
                w = qw[i : i + 1, :]
                weights[a, :, pl.ds(slot * local + i * 128, 128)] = (
                    column[0] * (xyz[0:1, lanes] * w)
                    + column[1] * (xyz[1:2, lanes] * w)
                    + column[2] * (xyz[2:3, lanes] * w)
                )

    fill_weights(0, coords, quad)
    for i in range(M // 128):
        lam[:, pl.ds(i * 128, 128)] = jnp.broadcast_to(rates[i : i + 1, :], (rows, 128))
    loads[-1].wait()

    pl.semaphore_wait(barrier, H * C + R + G - 1 + H - 1 - 2 * is_self.astype(jnp.int32))

    def first_copy(d, e):
        return pltpu.make_async_remote_copy(
            src_ref=start, dst_ref=landed.at[e, c], send_sem=first_send.at[d, e],
            recv_sem=first_recv.at[e, c], device_id=(H * (z ^ d) + (q ^ e), z),
            device_id_type=MESH,
        )

    for d in reversed(range(G)):
        for e in reversed(range(H)):
            unless(is_self & (d + e == 0), lambda d=d, e=e: first_copy(d, e).start())

    @pl.when(is_self)
    def _():
        pltpu.make_async_copy(start, landed.at[0, c], first_recv.at[0, c]).start()

    def to_core(e, src, dst, send, recv_sem):
        return pltpu.make_async_remote_copy(
            src_ref=src, dst_ref=dst, send_sem=send, recv_sem=recv_sem,
            device_id=(H * z + (q ^ e), c), device_id_type=MESH,
        )

    def geo_copy(e, which):
        src, dst = ((coords, coords_in), (quad, quad_in))[which]
        return to_core(
            e, src, dst.at[e - 1], geo_send.at[e - 1, which], geo_recv.at[e - 1, which]
        )

    def chunk_of(i):
        return pl.ds(*cuts[i])

    def slab_copy(e, i):
        lanes = chunk_of(i)
        return to_core(
            e, basis.at[pl.ds(0, local), lanes], basis.at[pl.ds(e * local, local), lanes],
            slab_send.at[e - 1, i], slab_recv.at[e - 1, i],
        )

    def node_copy(e):
        return to_core(
            e, nodes_out.at[e - 1], nodes_in.at[e - 1], node_send.at[e - 1], node_recv.at[e - 1]
        )

    for e in range(1, H):
        for which in range(2):
            geo_copy(e, which).start()
    ahead = chunks // 2
    for i in range(ahead):
        for e in range(1, H):
            slab_copy(e, i).start()
    for e in range(1, H):
        for which in range(2):
            geo_copy(e, which).wait_recv()
        fill_weights(e, coords_in.at[e - 1], quad_in.at[e - 1])

    part_id = lax.broadcasted_iota(jnp.int32, (rows, local), 0) // wl

    def scale(total, a, slot):
        lanes = pl.ds(slot * local, local)
        v = total * weights[a, :, lanes]
        turned = jnp.where(part_id == 0, pltpu.roll(v, rows - wl, 0), -pltpu.roll(v, wl, 0))
        scaled[:, lanes] = turned.astype(jnp.bfloat16)

    total = jnp.zeros((H * rows, local), jnp.float32)
    for d in range(C):
        s = c ^ d
        lanes = pl.ds(pl.multiple_of(s * width, width), width)
        for e in range(H):
            pltpu.make_async_copy(start, landed.at[e, s], first_recv.at[e, s]).wait()
            for x in range(2):
                field[pl.ds(e * rows + x * wl, wl), lanes] = landed[e, s, x].astype(jnp.float32)
        block = field[:, lanes].astype(jnp.bfloat16)
        cur[:, lanes] = block[:rows, :]
        total = total + lax.dot_general(
            block, basis[pl.ds(0, local), lanes], NT, preferred_element_type=jnp.float32
        )
    for e in range(1, H):
        nodes_out[e - 1] = total[e * rows : (e + 1) * rows, :]
        node_copy(e).start()
    for i in range(ahead, chunks):
        for e in range(1, H):
            slab_copy(e, i).start()
    scale(total[:rows, :], 0, 0)

    def part_copy(p, d, i):
        return pltpu.make_async_remote_copy(
            src_ref=parts.at[p, :, chunk_of(i)], dst_ref=recv.at[p, d - 1, :, chunk_of(i)],
            send_sem=part_send.at[p, d - 1, i], recv_sem=part_recv.at[p, d - 1, i],
            device_id=(H * (z ^ d) + q, c), device_id_type=MESH,
        )

    def send_part(p, i, block):
        parts[p, :, chunk_of(i)] = block.astype(jnp.bfloat16)
        for d in [1] + list(reversed(range(2, G))):
            part_copy(p, d, i).start()

    for i in range(chunks):
        early[:, chunk_of(i)] = lax.dot_general(
            scaled[:, pl.ds(0, local)], basis[pl.ds(0, local), chunk_of(i)], NN,
            preferred_element_type=jnp.float32,
        )
    for e in range(1, H):
        node_copy(e).wait_recv()
        scale(nodes_in[e - 1], 0, e)
    @pl.when(q != 0)
    def _():
        pl.semaphore_wait(turn, 1)

    for i in range(chunks):
        for e in range(1, H):
            slab_copy(e, i).wait_recv()
        send_part(0, i, early[:, chunk_of(i)] + lax.dot_general(
            scaled[:, pl.ds(local, (H - 1) * local)],
            basis[pl.ds(local, (H - 1) * local), chunk_of(i)], NN,
            preferred_element_type=jnp.float32,
        ))
    @pl.when(q != H - 1)
    def _():
        for d in range(1, G):
            part_copy(0, d, chunks - 1).wait_send()
        pl.semaphore_signal(
            turn, inc=1, device_id=(H * z + lax.rem(q + 1, H), c), device_id_type=MESH
        )

    def finish(step):
        p = lax.rem(step, 2)
        odd = p == 1
        factor = jnp.where(odd, 1.0, 0.5).astype(jnp.float32)
        for i in range(chunks):
            lanes = chunk_of(i)
            ready[:, lanes] = (
                field[pl.ds(0, rows), lanes]
                - (factor * lam[:, lanes]) * cur[:, lanes].astype(jnp.float32)
                + parts[p, :, lanes].astype(jnp.float32)
            )
        total = jnp.zeros((rows, H * local), jnp.float32)
        for i in range(chunks):
            lanes = chunk_of(i)
            acc = ready[:, lanes]
            for d in range(1, G):
                part_copy(p, d, i).wait_recv()
                acc = acc + recv[p, d - 1, :, lanes].astype(jnp.float32)
            rounded = acc.astype(jnp.bfloat16)
            cur[:, lanes] = rounded
            field[pl.ds(0, rows), lanes] = jnp.where(
                odd, rounded.astype(jnp.float32), field[pl.ds(0, rows), lanes]
            )
            total = total + lax.dot_general(
                rounded, basis[:, lanes], NT, preferred_element_type=jnp.float32
            )
        for slot in range(H):
            scale(total[:, slot * local : (slot + 1) * local], step + 1, slot)

    def sent(p, count):
        for i in range(count):
            for d in range(1, G):
                part_copy(p, d, i).wait_send()

    def half_step(step, carry):
        finish(step)
        p = lax.rem(step, 2)
        v = scaled[...]
        for i in range(chunks):
            send_part(1 - p, i, lax.dot_general(
                v, basis[:, chunk_of(i)], NN, preferred_element_type=jnp.float32
            ))
        sent(p, chunks - 1)

        @pl.when((step > 0) | (q == H - 1))
        def _():
            for d in range(1, G):
                part_copy(p, d, chunks - 1).wait_send()

        return carry

    lax.fori_loop(0, halves - 2, half_step, 0)
    finish(halves - 2)

    def last_copy(d):
        return pltpu.make_async_remote_copy(
            src_ref=lastout.at[d], dst_ref=lastin.at[z], send_sem=last_send.at[d],
            recv_sem=last_recv.at[z], device_id=(H * c + q, c ^ d), device_id_type=MESH,
        )

    v = scaled[...]
    for d in reversed(range(C)):
        lanes = pl.ds(pl.multiple_of((c ^ d) * width, width), width)
        rest = field[pl.ds(0, rows), lanes] - lam[:, lanes] * cur[:, lanes].astype(jnp.float32)
        block = lax.dot_general(v, basis[:, lanes], NN, preferred_element_type=jnp.float32)
        lastout[d] = (block + jnp.where(is_self, rest, 0.0)).astype(jnp.bfloat16)
        if d:
            last_copy(d).start()
    unless(is_self, lambda: last_copy(0).start())

    @pl.when(is_self)
    def _():
        pltpu.make_async_copy(lastout.at[0], lastin.at[z], last_recv.at[z]).start()

    fresh = jnp.zeros((rows, width), jnp.float32)
    for s in range(G):
        pltpu.make_async_copy(lastout.at[0], lastin.at[s], last_recv.at[s]).wait()
        fresh = fresh + lastin[s].astype(jnp.float32)
    for x in range(2):
        out[x] = fresh[x * wl : (x + 1) * wl, :].astype(jnp.bfloat16)

    sent((halves - 2) % 2, chunks)
    for d in range(C):
        unless(is_self & (d == 0), lambda d=d: last_copy(d).wait_send())
    for d in range(G):
        for e in range(H):
            unless(is_self & (d + e == 0), lambda d=d, e=e: first_copy(d, e).wait_send())
    for e in range(1, H):
        node_copy(e).wait_send()
        for which in range(2):
            geo_copy(e, which).wait_send()
        for i in range(chunks):
            slab_copy(e, i).wait_send()


def on_device(R, C, basis, coords, quad, magnetization, rates, dirs):
    H = R // C
    G = R // H
    local, M = basis.shape
    start = jnp.transpose(magnetization, (0, 2, 1))
    quad = quad.reshape(-1, 128)
    rates = rates.reshape(-1, 128)
    _, wl, width = start.shape
    rows = 2 * wl
    cuts = cuts_of(M)
    chunks = len(cuts)
    dma = pltpu.SemaphoreType.DMA
    bf16, f32 = jnp.bfloat16, jnp.float32
    result = pl.pallas_call(
        functools.partial(kernel, R, C),
        out_shape=pltpu.VMEM(start.shape, bf16),
        in_specs=[pl.BlockSpec(memory_space=pl.ANY)] * 6,
        out_specs=pl.BlockSpec(memory_space=pltpu.VMEM),
        scratch_shapes=[
            pltpu.VMEM((H * local, M), bf16),
            pltpu.VMEM(coords.shape, f32),
            pltpu.VMEM(quad.shape, f32),
            pltpu.VMEM(rates.shape, f32),
            pltpu.VMEM(dirs.shape, f32),
            pltpu.VMEM((H, C, 2, wl, width), bf16),
            pltpu.VMEM((rows, M), bf16),
            pltpu.VMEM((H * rows, M), f32),
            pltpu.VMEM((rows, M), f32),
            pltpu.VMEM((rows, M), f32),
            pltpu.VMEM((rows, M), f32),
            pltpu.VMEM((2, rows, M), bf16),
            pltpu.VMEM((2, G - 1, rows, M), bf16),
            pltpu.VMEM((2 * STEPS, rows, H * local), f32),
            pltpu.VMEM((H - 1,) + coords.shape, f32),
            pltpu.VMEM((H - 1,) + quad.shape, f32),
            pltpu.VMEM((H - 1, rows, local), f32),
            pltpu.VMEM((H - 1, rows, local), f32),
            pltpu.VMEM((rows, H * local), bf16),
            pltpu.VMEM((C, rows, width), bf16),
            pltpu.VMEM((G, rows, width), bf16),
            dma((5,)),
            dma((H - 1, chunks)), dma((H - 1, chunks)),
            dma((H - 1, 2)), dma((H - 1, 2)),
            dma((G, H)), dma((H, C)),
            dma((H - 1,)), dma((H - 1,)),
            pltpu.SemaphoreType.REGULAR,
            dma((2, G - 1, chunks)), dma((2, G - 1, chunks)),
            dma((C,)), dma((G,)),
        ],
        compiler_params=pltpu.CompilerParams(collective_id=0, has_side_effects=True),
    )(basis, coords, quad, start, rates, dirs)
    return jnp.transpose(result, (0, 2, 1))


def solution(mesh):
    return jax.shard_map(
        functools.partial(on_device, mesh.shape["row"], mesh.shape["col"]),
        mesh=mesh,
        in_specs=(P("row", None), P(None, "row"), P("row"), P(None, "col", "row"), P(), P()),
        out_specs=P(None, "col", "row"),
        check_vma=False,
    )
```
